256 devices in a mesh: gx: 32 (over z, y_lo, core), gz: 8 (over y_hi, x).
Axes of the slice: x: 4, y: 4 (y_hi: 2, y_lo: 2; y = y_hi * 2 + y_lo), z: 8, core: 2. Of those that a mesh axis runs over, the one named last changes fastest.
Arguments:
- bins: float32 [256, 33, 8, 4096], P('gz', None, None, 'gx'), may hold values from 0.05 to 1
- u_courant: float32 [256, 8, 4096], P('gz', None, 'gx'), may hold values from -0.3 to 0.3
- w_courant: float32 [256, 8, 4096], P('gz', None, 'gx'), may hold values from -0.15 to 0.15
- fall_courant: float32 [33], replicated, may hold values from 0.01 to 0.2
- kernel: float32 [33, 33], replicated, may hold values from 0.005 to 0.05
- redistribution: float32 [33, 33], replicated, may hold values from -1 to 1
- block_ids: int32 [8, 2048], P('gz', 'gx'), may hold values from 0 to 63, as said below
- block_counts: int32 [8, 32], P('gz', 'gx'), may hold values from 1 to 32, 512 in all within a row
- block_inverse: float32 [256, 32, 4096], P('gz', None, 'gx'), may hold values from -0.5 to 0.6
Outputs:
- next_bins: float32 [256, 33, 8, 4096], P('gz', None, None, 'gx')
- pressure: float32 [256, 8, 4096], P('gz', None, 'gx')
The draws below stay inside these ranges and needn't reach their ends.
Inputs may be any that keep to these rules, and one draw needn't show every extreme that they name: `block_ids`: each device's 64 entries are a permutation of 0 .. 63. `block_counts`: along gx the counts of one gz index sum to exactly 64 * 32 // 4, and one device holds 32.
All inputs are finite; a program needn't handle non-finite values.
Results may differ from the reference program's by a relative error of at most 0.0001.
Values sent between devices are 32-bit elements; how exact they have to be, the bound alone decides.
A program may use at most 128 MiB of HBM per device.

```python
import math
import jax
import jax.numpy as jnp
import numpy as np
from jax import lax

BINS = 33
BLOCK = 8
ITERS = 4
CZ = 32
NY = 8
CX = 128
NZ = 256
NX = 4096
BLK_DEV = 64
N_GX = 32
N_GZ = 8


def draw_block_ids(key, part):
    scores = jax.random.randint(jax.random.fold_in(key, 5), (N_GZ, N_GX, BLK_DEV), 0, 1 << 16)
    scores = scores * BLK_DEV + jnp.arange(BLK_DEV, dtype=jnp.int32)[None, None, :]
    order = jnp.argsort(scores, axis=-1, stable=True).astype(jnp.int32)
    return order.reshape(N_GZ, N_GX * BLK_DEV)


def draw_block_inverse(key, part):
    first_key, second_key = jax.random.split(jax.random.fold_in(key, 11))
    diagonal = jax.random.uniform(first_key, (NZ, CZ, NX), jnp.float32, 0.3, 0.6)
    coupling = jnp.clip(0.1 * jax.random.normal(second_key, (NZ, CZ, NX), jnp.float32), -0.5, 0.5)
    on_diagonal = jnp.arange(NZ)[:, None] % CZ == jnp.arange(CZ)[None, :]
    return jnp.where(on_diagonal[:, :, None], diagonal, coupling).astype(jnp.float32)


def block_levels(key, shape, shards, low, largest):
    factor_of = 1.0
    for dim, parts in shards:
        steps = jax.random.uniform(jax.random.fold_in(jax.random.fold_in(key, 6), dim), (parts,), jnp.float32, low / len(shards), largest / len(shards))
        factor_of = factor_of * jnp.repeat(jnp.exp(steps), shape[dim] // parts).reshape((-1,) + (1,) * (len(shape) - 1 - dim))
    return factor_of


def profile(amount, total, bound, lean):
    loads = [(1 << 20) // math.isqrt(grade ** lean) + 1 for grade in range(2, amount + 1)]
    surplus, counts = total - bound - (amount - 1), [1] * (amount - 1)
    while surplus > 0:
        movable = [i for i in range(amount - 1) if counts[i] < bound]
        pool, remaining = sum([loads[i] for i in movable]), surplus
        for i in movable:
            addition = min(bound - counts[i], max(1, remaining * loads[i] // pool), surplus)
            counts[i] = counts[i] + addition
            surplus = surplus - addition
    return np.array([bound] + counts)


def ragged(own_key, amount, total, bound, slope):
    if amount == 2:
        one = jax.random.randint(own_key, (), max(1, total - bound), min(bound, total - 1) + 1)
        return jnp.stack([one, total - one])
    sizes = jnp.asarray(profile(amount, total, bound, slope), jnp.int32)
    twos = (amount - 1) // 2
    source_of, receiver = sizes[1:1 + 2 * twos:2], sizes[2:2 + 2 * twos:2]
    slack = jnp.minimum(source_of - 1, bound - receiver)
    passed = jax.random.randint(jax.random.fold_in(own_key, 1), (twos,), 0, 1 << 20) % (slack + 1)
    sizes = sizes.at[1:1 + 2 * twos:2].set(source_of - passed).at[2:2 + 2 * twos:2].set(receiver + passed)
    return sizes[jax.random.permutation(jax.random.fold_in(own_key, 2), amount)]


def noise(rng, dims, deviation, limit, held_as=jnp.bfloat16):
    entries = deviation * jax.random.normal(rng, dims, jnp.float32)
    return jnp.clip(entries, min=-limit, max=limit).astype(held_as)


def setup_inputs(seed: int = 0) -> dict:
    seeds = jax.random.split(jax.random.key(seed), 10)
    bins = jnp.clip(jnp.exp(math.log(1.0) - 2.9957323 * jax.random.uniform(seeds[0], (NZ, BINS, NY, NX), jnp.float32) ** block_levels(seeds[0], (NZ, BINS, NY, NX), ((0, 8), (3, 32)), -0.2, 0.2)), 0.05, 1.0)
    u_courant = jnp.clip(jax.random.uniform(seeds[1], (NZ, NY, NX), jnp.float32, -0.3, 0.3) * block_levels(seeds[1], (NZ, NY, NX), ((0, 8), (2, 32)), -0.4, 0.0), -0.3, 0.3)
    w_courant = jnp.clip(jax.random.uniform(seeds[2], (NZ, NY, NX), jnp.float32, -0.15, 0.15) * block_levels(seeds[2], (NZ, NY, NX), ((0, 8), (2, 32)), -0.4, 0.0), -0.15, 0.15)
    fall_courant = jnp.clip(jnp.exp(jax.random.uniform(seeds[3], (BINS,), jnp.float32, math.log(0.01), math.log(0.2))), 0.01, 0.2)
    kernel = jnp.clip(jnp.exp(jax.random.uniform(seeds[4], (BINS, BINS), jnp.float32, math.log(0.005), math.log(0.05))), 0.005, 0.05)
    redistribution = noise(seeds[5], (BINS, BINS), BINS ** -0.5, 1.0, jnp.float32)
    block_ids = draw_block_ids(jax.random.fold_in(seeds[9], 71), 0)
    block_counts = jax.vmap(lambda own: ragged(own, N_GX, BLK_DEV * N_GX // 4, BLK_DEV // 2, 2))(jax.random.split(seeds[7], N_GZ)).reshape((N_GZ, N_GX)).astype(jnp.int32)
    block_inverse = draw_block_inverse(jax.random.fold_in(seeds[9], 71), 0)
    return {"bins": bins, "u_courant": u_courant, "w_courant": w_courant, "fall_courant": fall_courant, "kernel": kernel, "redistribution": redistribution, "block_ids": block_ids, "block_counts": block_counts, "block_inverse": block_inverse}


def reference(bins, u_courant, w_courant, fall_courant, kernel, redistribution, block_ids, block_counts, block_inverse):
    precise = lax.Precision.HIGHEST
    levels, bin_count, rows_y, columns = bins.shape
    right_cells = jnp.roll(bins, -1, axis=3)
    x_speed = u_courant[:, None]
    flux_x = jnp.maximum(x_speed, 0.0) * bins + jnp.minimum(x_speed, 0.0) * right_cells
    flux_left = jnp.roll(flux_x, 1, axis=3)
    zero_layer = jnp.zeros((1, bin_count, rows_y, columns), bins.dtype)
    padded = jnp.concatenate([zero_layer, bins, zero_layer], axis=0)
    w_padded = jnp.concatenate([jnp.zeros((1, rows_y, columns), w_courant.dtype), w_courant], axis=0)
    vertical = w_padded[:, None] - fall_courant[None, :, None, None]
    flux_z = jnp.maximum(vertical, 0.0) * padded[:-1] + jnp.minimum(vertical, 0.0) * padded[1:]
    advected = bins - (flux_x - flux_left) - (flux_z[1:] - flux_z[:-1])

    block_list = block_ids.reshape(N_GZ, N_GX, BLK_DEV)
    slot_range = jnp.arange(BLK_DEV, dtype=jnp.int32)
    is_live = slot_range[None, None, :] < block_counts[:, :, None]
    matches = (block_list[..., :, None] == slot_range[None, None, None, :]) & is_live[..., None]
    cloudy = jnp.sum(jnp.where(matches, 1.0, 0.0), axis=2).astype(bins.dtype)
    z_blocks, y_blocks, x_blocks = CZ // BLOCK, NY // BLOCK, CX // BLOCK
    cloudy = cloudy.reshape(N_GZ, N_GX, z_blocks, y_blocks, x_blocks)

    def collide_level(item):
        field, marks = item
        cells = jnp.broadcast_to(marks.transpose(1, 2, 0, 3)[:, None, :, None, :, :, None],
                                 (z_blocks, BLOCK, y_blocks, BLOCK, N_GX, x_blocks, BLOCK)).reshape(CZ, rows_y, columns)
        growth_rate = jnp.einsum("zayx,ab->zbyx", field, kernel, precision=precise)
        tendency = jnp.einsum("zayx,ab->zbyx", field * growth_rate, redistribution, precision=precise)
        return field + tendency * cells[:, None]

    next_bins = lax.map(collide_level, (advected.reshape(N_GZ, CZ, bin_count, rows_y, columns), cloudy))
    next_bins = next_bins.reshape(levels, bin_count, rows_y, columns)

    below_w = jnp.concatenate([jnp.zeros((1, rows_y, columns), w_courant.dtype), w_courant[:-1]], axis=0)
    divergence = (u_courant - jnp.roll(u_courant, 1, axis=2)) + (w_courant - below_w)
    spectrum = jnp.fft.fft(divergence, axis=2)
    source_term = jnp.stack([jnp.real(spectrum), jnp.imag(spectrum)]).astype(bins.dtype).reshape(2, N_GZ, CZ, rows_y, columns)
    inverse_blocks = block_inverse.reshape(N_GZ, CZ, CZ, columns)
    solved = jnp.zeros_like(source_term)
    for sweep in range(ITERS):
        source = source_term
        if sweep > 0:
            edge_zero = jnp.zeros((2, 1, rows_y, columns), bins.dtype)
            above = jnp.concatenate([solved[:, 1:, 0], edge_zero], axis=1)
            below = jnp.concatenate([edge_zero, solved[:, :-1, CZ - 1]], axis=1)
            source = source.at[:, :, CZ - 1].add(above)
            source = source.at[:, :, 0].add(below)
        solved = jnp.einsum("gijk,cgjyk->cgiyk", inverse_blocks, source, precision=precise)
    solved = solved.reshape(2, levels, rows_y, columns)
    pressure = jnp.real(jnp.fft.ifft(solved[0] + 1j * solved[1], axis=2)).astype(bins.dtype)
    return next_bins, pressure
```

```python
import functools
import math

import jax
import jax.numpy as jnp
import numpy as np
from jax import lax
from jax.experimental import pallas as pl
from jax.experimental.pallas import tpu as pltpu
from jax.sharding import PartitionSpec as P

F32 = jnp.float32
BF16 = jnp.bfloat16
MESH = pl.DeviceIdType.MESH
NB = 33
NBP = 48
NL = 32
NG = 8
NP = 32
LVL = NB * 8


def halves(x):
    hi = np.asarray(np.asarray(x, np.float32), jnp.bfloat16)
    lo = np.asarray(np.asarray(x - hi.astype(np.float64), np.float32), jnp.bfloat16)
    return hi, lo


def tables():
    p = np.arange(32)
    c = np.arange(128)
    pj = 2.0 * math.pi / 32 * (p[:, None] * c[None, :] % 32)
    cj = 2.0 * math.pi / 4096 * (c[:, None] * c[None, :])
    cos, sin = np.cos(pj), np.sin(pj)
    e_hi, e_lo = halves(np.concatenate([cos, -sin], 1))
    e3 = np.concatenate([e_hi, e_hi, e_lo], 0)
    fwd = np.concatenate([np.concatenate([cos, sin], 1), np.concatenate([-sin, cos], 1)], 0)
    f2 = np.concatenate(halves(fwd), 0)
    g = np.concatenate([np.concatenate([cos, sin], 1), np.concatenate([-sin, cos], 1)], 0)
    g_hi, g_lo = halves(g)
    g3 = np.concatenate([g_hi, g_hi, g_lo], 0)
    h2 = np.concatenate(halves(np.concatenate([cos, -sin], 1) / 4096.0), 0)
    mats = np.concatenate([e3, f2, g3, h2], 0)
    tw = np.concatenate([np.cos(cj), -np.sin(cj)], 1).astype(np.float32)
    return mats, tw


def split(x):
    hi = x.astype(BF16)
    lo = (x - hi.astype(F32)).astype(BF16)
    return hi, lo


def dot(a, b):
    return jnp.dot(a, b, preferred_element_type=F32)


def dot_t(a, b):
    return lax.dot_general(a, b, (((0,), (0,)), ((), ())), preferred_element_type=F32)


def kernel_body(
    bins_h, u_h, w_h, binv_h, mats_h, tw_h, coll_h, ids_v, fall_s, cnt_s,
    out_h, pres_h,
    bins_v, out_v, u_v, w_v, binv_v, mats_v, tw_v, coll_v,
    send1, x1, send2, x2, send3, x3, send4, ybuf,
    esend, edges, csend, corners, bpad, tpad,
    whalo, zlo, zhi, send_f, send_l, send_u, halo_r, halo_l, halo_u, prior,
    adv, fz, mask_v,
    in_sem, bin_sem, out_sem, p_sem,
    a2a_send, a2a_recv, e_send, e_recv, c_send, c_recv, h_send, h_recv,
):
    me = lax.axis_index("gx")
    g = lax.axis_index("gz")
    right = {"gx": lax.rem(me + 1, NP)}
    left = {"gx": lax.rem(me + NP - 1, NP)}
    above = {"gz": lax.rem(g + 1, NG)}
    below = {"gz": lax.rem(g + NG - 1, NG)}

    lane = lax.broadcasted_iota(jnp.int32, (8, 128), 1)
    sub = lax.broadcasted_iota(jnp.int32, (8, 128), 0)

    barrier = pltpu.get_barrier_semaphore()

    def greet_x(o, _):
        pl.semaphore_signal(barrier, inc=1, device_id={"gx": lax.rem(me + o, NP)}, device_id_type=MESH)
        return 0

    def greet_z(o, _):
        pl.semaphore_signal(barrier, inc=1, device_id={"gz": lax.rem(g + o, NG)}, device_id_type=MESH)
        return 0

    lax.fori_loop(1, NP, greet_x, 0)
    lax.fori_loop(1, NG, greet_z, 0)

    loads = [
        pltpu.make_async_copy(s, d, in_sem.at[i])
        for i, (s, d) in enumerate(
            [(u_h, u_v), (w_h, w_v), (binv_h, binv_v), (mats_h, mats_v), (tw_h, tw_v), (coll_h, coll_v)]
        )
    ]
    loads[0].start()
    loads[1].start()
    bin_loads = [
        pltpu.make_async_copy(bins_h.at[pl.ds(i * 4 * LVL, 4 * LVL)], bins_v.at[pl.ds(i * 4 * LVL, 4 * LVL)], bin_sem.at[i])
        for i in range(8)
    ]
    for i in range(8):
        bin_loads[i].start()
    for c in loads[2:]:
        c.start()
    loads[0].wait()
    loads[1].wait()

    def tile_div(q, w_under):
        u = u_v[pl.ds(q * 8, 8), :]
        before = jnp.where(lane == 0, 0.0, pltpu.roll(u, 1, 1))
        d = (u - before) + (w_v[pl.ds(q * 8, 8), :] - w_under)
        row = jnp.sum(jnp.where(lane == sub, jnp.broadcast_to(u[:, 127:128], (8, 128)), 0.0), axis=0, keepdims=True)
        send1[pl.ds(q * 16, 8), :] = d
        send1[pl.ds(q * 16 + 8, 8), :] = jnp.broadcast_to(row, (8, 128))

    tile_div(0, jnp.zeros((8, 128), F32))

    def div_step(q, _):
        tile_div(q, w_v[pl.ds(q * 8 - 8, 8), :])
        return 0

    lax.fori_loop(1, NL, div_step, 0)

    pl.semaphore_wait(barrier, NP - 1 + NG - 1)

    w_copy = pltpu.make_async_remote_copy(
        src_ref=w_v.at[pl.ds(248, 8)], dst_ref=whalo, send_sem=h_send.at[0], recv_sem=h_recv.at[0],
        device_id=above, device_id_type=MESH)
    w_copy.start()

    def msg(stage, src, dst, rows, peer, at):
        s0 = pl.multiple_of(peer * at, 8)
        d0 = pl.multiple_of(me * at, 8)
        return pltpu.make_async_remote_copy(
            src_ref=src.at[pl.ds(s0, rows)], dst_ref=dst.at[pl.ds(d0, rows)],
            send_sem=a2a_send.at[stage, peer], recv_sem=a2a_recv.at[stage, me],
            device_id={"gx": peer}, device_id_type=MESH)

    def peer_of(t):
        half = (t + 1) // 2
        odd = lax.rem(t, 2)
        o = 16 + odd * half - (1 - odd) * half
        return lax.rem(me + o, NP)

    def send_all(stage, src, dst, rows, at, skip=False):
        def step(t, _):
            peer = peer_of(t)
            if skip:
                @pl.when(peer != 0)
                def _():
                    msg(stage, src, dst, rows, peer, at).start()
            else:
                msg(stage, src, dst, rows, peer, at).start()
            return 0
        lax.fori_loop(0, NP - 1, step, 0)

    def wait_all(stage, src, dst, rows, at):
        def step(t, _):
            peer = lax.rem(me + t + 1, NP)
            d0 = pl.multiple_of(peer * at, 8)
            pltpu.make_async_remote_copy(
                src_ref=src.at[pl.ds(d0, rows)], dst_ref=dst.at[pl.ds(d0, rows)],
                send_sem=a2a_send.at[stage, peer], recv_sem=a2a_recv.at[stage, peer],
                device_id={"gx": peer}, device_id_type=MESH).wait()
            return 0
        lax.fori_loop(0, NP - 1, step, 0)

    def own(src, dst, rows, at):
        m0 = pl.multiple_of(me * at, 8)
        dst[pl.ds(m0, rows), :] = src[pl.ds(m0, rows), :]

    send_all(0, send1, x1, 9, 16, skip=True)

    bin_loads[7].wait()
    bin_loads[0].wait()
    z_up = pltpu.make_async_remote_copy(
        src_ref=bins_v.at[pl.ds(31 * LVL, LVL)], dst_ref=zlo, send_sem=h_send.at[1], recv_sem=h_recv.at[1],
        device_id=above, device_id_type=MESH)
    z_down = pltpu.make_async_remote_copy(
        src_ref=bins_v.at[pl.ds(0, LVL)], dst_ref=zhi, send_sem=h_send.at[2], recv_sem=h_recv.at[2],
        device_id=below, device_id_type=MESH)
    z_up.start()
    z_down.start()

    w_copy.wait()
    not_first = g > 0
    send1[pl.ds(0, 8), :] = send1[pl.ds(0, 8), :] - jnp.where(not_first, whalo[...], 0.0)

    @pl.when(me != 0)
    def _():
        msg(0, send1, x1, 9, me * 0, 16).start()

    own(send1, x1, 16, 16)

    loads[2].wait()
    csend[...] = jnp.zeros((8, 128), F32)
    for i, r in enumerate((0, 31, 31 * 32, 31 * 32 + 31)):
        csend[pl.ds(i, 1), :] = binv_v[pl.ds(r, 1), :]

    def z_msg(src, dst, rows, peer, ss, rs):
        d0 = pl.multiple_of(g * rows, 8)
        return pltpu.make_async_remote_copy(
            src_ref=src, dst_ref=dst.at[pl.ds(d0, rows)], send_sem=ss.at[peer], recv_sem=rs.at[g],
            device_id={"gz": peer}, device_id_type=MESH)

    def send_z(src, dst, rows, ss, rs):
        def step(o, _):
            z_msg(src, dst, rows, lax.rem(g + o, NG), ss, rs).start()
            return 0
        lax.fori_loop(1, NG, step, 0)
        dst[pl.ds(pl.multiple_of(g * rows, 8), rows), :] = src[...]

    def wait_z(src, dst, rows, ss, rs):
        def step(o, _):
            peer = lax.rem(g + o, NG)
            pltpu.make_async_remote_copy(
                src_ref=src, dst_ref=dst.at[pl.ds(pl.multiple_of(peer * rows, 8), rows)], send_sem=ss.at[peer], recv_sem=rs.at[peer],
                device_id={"gz": peer}, device_id_type=MESH).wait()
            return 0
        lax.fori_loop(1, NG, step, 0)

    send_z(csend, corners, 8, c_send, c_recv)

    for i in range(1, 7):
        bin_loads[i].wait()

    def pack(i, _):
        first = jnp.zeros((8, 128), F32)
        last = jnp.zeros((8, 128), F32)
        for r in range(2):
            for m in range(NB):
                v = bins_v[pl.ds((2 * i + r) * LVL + m * 8, 8), :]
                hit = lane == (NB * r + m)
                first = jnp.where(hit, jnp.broadcast_to(v[:, 0:1], (8, 128)), first)
                last = jnp.where(hit, jnp.broadcast_to(v[:, 127:128], (8, 128)), last)
        speeds = jnp.where(
            lane < NB,
            jnp.broadcast_to(u_v[pl.ds(i * 16, 8), :][:, 127:128], (8, 128)),
            jnp.broadcast_to(u_v[pl.ds(i * 16 + 8, 8), :][:, 127:128], (8, 128)))
        send_f[pl.ds(i * 8, 8), :] = first
        send_l[pl.ds(i * 8, 8), :] = last
        send_u[pl.ds(i * 8, 8), :] = speeds
        return 0

    lax.fori_loop(0, NL // 2, pack, 0)
    x_copies = [
        pltpu.make_async_remote_copy(src_ref=s, dst_ref=d, send_sem=h_send.at[i], recv_sem=h_recv.at[i], device_id=to, device_id_type=MESH)
        for i, s, d, to in ((3, send_f, halo_r, left), (4, send_l, halo_l, right), (5, send_u, halo_u, right))
    ]
    for c in x_copies:
        c.start()

    block = lax.broadcasted_iota(jnp.int32, (64, 64), 0)
    slot = lax.broadcasted_iota(jnp.int32, (64, 64), 1)
    hits = (jnp.broadcast_to(ids_v[...], (64, 64)) == block) & (slot < cnt_s[0, 0])
    marks = jnp.max(jnp.where(hits, 1.0, 0.0), axis=1, keepdims=True)
    col_block = lax.broadcasted_iota(jnp.int32, (16, 128), 1) // 8
    row_block = lax.broadcasted_iota(jnp.int32, (16, 128), 0)
    for bz in range(4):
        wide = jnp.broadcast_to(marks[bz * 16:bz * 16 + 16, :], (16, 128))
        mask_v[pl.ds(bz, 1), :] = jnp.sum(jnp.where(col_block == row_block, wide, 0.0), axis=0, keepdims=True)

    adv[...] = jnp.zeros((NBP * 8, 128), F32)
    for c in loads[3:]:
        c.wait()

    z_up.wait()
    z_down.wait()
    for c in x_copies:
        c.wait()

    def prior_step(i, _):
        s = pl.ds(i * 8, 8)
        speed = halo_u[s, :]
        prior[s, :] = jnp.maximum(speed, 0.0) * halo_l[s, :] + jnp.minimum(speed, 0.0) * send_f[s, :]
        return 0

    lax.fori_loop(0, NL // 2, prior_step, 0)

    not_last = g < NG - 1
    w_low = jnp.where(not_first, whalo[...], 0.0)

    def low_face(m, _):
        s = pl.ds(m * 8, 8)
        c = w_low - fall_s[m]
        fz[s, :] = jnp.maximum(c, 0.0) * jnp.where(not_first, zlo[s, :], 0.0) + jnp.minimum(c, 0.0) * bins_v[s, :]
        bins_v[pl.ds(NL * LVL + m * 8, 8), :] = jnp.where(not_last, zhi[s, :], 0.0)
        return 0

    lax.fori_loop(0, NB, low_face, 0)

    def level(z, i, r):
        u = u_v[pl.ds(z * 8, 8), :]
        u_pos, u_neg = jnp.maximum(u, 0.0), jnp.minimum(u, 0.0)
        w = w_v[pl.ds(z * 8, 8), :]
        hr = halo_r[pl.ds(i * 8, 8), :]
        pf = prior[pl.ds(i * 8, 8), :]
        base = z * LVL
        for m in range(NB):
            k = NB * r + m
            b = bins_v[pl.ds(base + m * 8, 8), :]
            up = bins_v[pl.ds(base + LVL + m * 8, 8), :]
            nxt = jnp.where(lane == 127, jnp.broadcast_to(hr[:, k:k + 1], (8, 128)), pltpu.roll(b, 127, 1))
            flux = u_pos * b + u_neg * nxt
            prev = jnp.where(lane == 0, jnp.broadcast_to(pf[:, k:k + 1], (8, 128)), pltpu.roll(flux, 1, 1))
            c = w - fall_s[m]
            top = jnp.maximum(c, 0.0) * b + jnp.minimum(c, 0.0) * up
            s = pl.ds(m * 8, 8)
            adv[s, :] = b - (flux - prev) - (top - fz[s, :])
            fz[s, :] = top
        mark = jnp.broadcast_to(mask_v[pl.ds(z // 8, 1), :], (NBP, 128))
        grow_w = coll_v[pl.ds(0, NBP), :]
        redi_w = coll_v[pl.ds(NBP, NBP), :]
        for h in range(4):
            ys = (2 * h, 2 * h + 1)
            v = jnp.concatenate([adv[pl.ds(y, NBP, stride=8), :] for y in ys], axis=1)
            hi, lo = split(v)
            rate = dot(grow_w, jnp.concatenate([hi, hi, lo], axis=0))
            hi, lo = split(v * rate)
            tend = dot(redi_w, jnp.concatenate([hi, hi, lo], axis=0))
            for n, y in enumerate(ys):
                part = slice(128 * n, 128 * n + 128)
                new = v[:, part] + tend[:, part] * mark
                out_v[pl.ds(base + y, NB, stride=8), :] = new[:NB]

    def flush(z2):
        s = pl.ds(z2 * 2 * LVL, 2 * LVL)
        return pltpu.make_async_copy(out_v.at[s], out_h.at[s], out_sem.at[z2])

    def levels(first, last):
        def step(i, _):
            level(2 * i, i, 0)
            level(2 * i + 1, i, 1)
            flush(i).start()
            return 0
        lax.fori_loop(first, last, step, 0)

    levels(0, CUT[0])

    wait_all(0, send1, x1, 9, 16)
    borders = x1[pl.ds(8, NP, stride=16), :]
    borders = pltpu.roll(borders, 1, 0)
    lane32 = lax.broadcasted_iota(jnp.int32, (32, 128), 1)
    e3 = mats_v[pl.ds(0, 96), :]
    f2 = mats_v[pl.ds(96, 128), :]
    twr = tw_v[:, 0:128]
    twi = tw_v[:, 128:256]
    for h in range(4):
        us = []
        for y in (2 * h, 2 * h + 1):
            xy = x1[pl.ds(y, NP, stride=16), :]
            shifted = borders if y == 0 else pltpu.roll(borders, 128 - y, 1)
            xy = xy - jnp.where(lane32 == 0, shifted, 0.0)
            hi, lo = split(xy)
            yy = dot_t(jnp.concatenate([hi, lo, hi], axis=0), e3)
            yr, yi = yy[:, :128], yy[:, 128:]
            us.append(jnp.concatenate([yr * twr - yi * twi, yr * twi + yi * twr], axis=0))
        hi, lo = split(jnp.concatenate(us, axis=1))
        both = dot(f2, hi)
        spec = both[:64] + both[64:] + dot(f2[:64], lo)
        for n, y in enumerate((2 * h, 2 * h + 1)):
            part = slice(128 * n, 128 * n + 128)
            send2[pl.ds(y, NP, stride=16), :] = spec[:32, part]
            send2[pl.ds(8 + y, NP, stride=16), :] = spec[32:, part]
    send_all(1, send2, x2, 16, 16)
    own(send2, x2, 16, 16)

    levels(CUT[0], CUT[1])

    wait_all(1, send2, x2, 16, 16)

    def apply_rows(rows):
        accs = [None] * len(rows)
        for j in range(NL):
            s = x2[pl.ds(j * 16, 16), :]
            for n, i in enumerate(rows):
                b = jnp.broadcast_to(binv_v[pl.ds(i * 32 + j, 1), :], (16, 128))
                accs[n] = b * s if accs[n] is None else accs[n] + b * s
        return accs

    low, high = apply_rows((0, 31))
    esend[pl.ds(0, 16), :] = low
    esend[pl.ds(16, 16), :] = high
    send_z(esend, edges, 32, e_send, e_recv)

    def solve_step(t, _):
        rows = [t * 4 + n for n in range(4)]
        for i, acc in zip(rows, apply_rows(rows)):
            send3[pl.ds(i * 16, 16), :] = acc
        return 0

    lax.fori_loop(0, NL // 4, solve_step, 0)
    wait_z(csend, corners, 8, c_send, c_recv)
    wait_z(esend, edges, 32, e_send, e_recv)

    zero = jnp.zeros((16, 128), F32)
    e0 = [edges[pl.ds(k * 32, 16), :] for k in range(NG)]
    e1 = [edges[pl.ds(k * 32 + 16, 16), :] for k in range(NG)]

    def corner(k, i):
        return jnp.broadcast_to(corners[pl.ds(k * 8 + i, 1), :], (16, 128))

    bs, ts = e0, e1
    for _ in range(2):
        nb, nt = [], []
        for k in range(NG):
            over = bs[k + 1] if k < NG - 1 else zero
            under = ts[k - 1] if k > 0 else zero
            nb.append(e0[k] + corner(k, 1) * over + corner(k, 0) * under)
            nt.append(e1[k] + corner(k, 3) * over + corner(k, 2) * under)
        bs, ts = nb, nt
    for k in range(NG):
        bpad[pl.ds(k * 16, 16), :] = bs[k]
        tpad[pl.ds(k * 16 + 16, 16), :] = ts[k]
    bpad[pl.ds(NG * 16, 16), :] = zero
    tpad[pl.ds(0, 16), :] = zero
    over = bpad[pl.ds(pl.multiple_of(g * 16 + 16, 8), 16), :]
    under = tpad[pl.ds(pl.multiple_of(g * 16, 8), 16), :]

    def update(i, _):
        s = pl.ds(i * 16, 16)
        top = jnp.broadcast_to(binv_v[pl.ds(i * 32 + 31, 1), :], (16, 128))
        bot = jnp.broadcast_to(binv_v[pl.ds(i * 32, 1), :], (16, 128))
        send3[s, :] = send3[s, :] + top * over + bot * under
        return 0

    lax.fori_loop(0, NL, update, 0)
    send_all(2, send3, x3, 16, 16)
    own(send3, x3, 16, 16)

    levels(CUT[1], CUT[2])

    wait_all(2, send3, x3, 16, 16)
    g3 = mats_v[pl.ds(224, 192), :]
    h2 = mats_v[pl.ds(416, 64), :]
    for h in range(4):
        zs = []
        for y in (2 * h, 2 * h + 1):
            s2 = jnp.concatenate([x3[pl.ds(y, NP, stride=16), :], x3[pl.ds(8 + y, NP, stride=16), :]], axis=0)
            hi, lo = split(s2)
            vv = dot_t(jnp.concatenate([hi, lo, hi], axis=0), g3)
            vr, vi = vv[:, :128], vv[:, 128:]
            zs.append(jnp.concatenate([vr * twr + vi * twi, vi * twr - vr * twi], axis=0))
        hi, lo = split(jnp.concatenate(zs, axis=1))
        both = dot(h2, hi)
        pr = both[:32] + both[32:] + dot(h2[:32], lo)
        for n, y in enumerate((2 * h, 2 * h + 1)):
            send4[pl.ds(y, NP, stride=8), :] = pr[:, 128 * n:128 * n + 128]
    send_all(3, send4, pres_h, 8, 8)
    m0 = pl.multiple_of(me * 8, 8)
    own_copy = pltpu.make_async_copy(send4.at[pl.ds(m0, 8)], pres_h.at[pl.ds(m0, 8)], p_sem)
    own_copy.start()

    levels(CUT[2], NL // 2)
    own_copy.wait()

    def drain(i, _):
        flush(i).wait()
        return 0

    lax.fori_loop(0, NL // 2, drain, 0)
    wait_all(3, send4, pres_h, 8, 8)


CUT = (4, 10, 16)


def body(bins, u, w, fall, kern, redi, ids, counts, binv):
    def stacked(m):
        m = jnp.pad(m.T, ((0, NBP - NB), (0, NBP - NB)))
        hi = lax.reduce_precision(m, 8, 7)
        return jnp.concatenate([hi, m - hi, hi], axis=1)

    coll = jnp.concatenate([stacked(kern), stacked(redi)], axis=0).astype(BF16)
    mats, tw = tables()
    vmem = lambda rows, cols=128, t=F32: pltpu.VMEM((rows, cols), t)
    dma = pltpu.SemaphoreType.DMA
    out, pres = pl.pallas_call(
        kernel_body,
        out_shape=(jax.ShapeDtypeStruct((NL * LVL, 128), F32), jax.ShapeDtypeStruct((NL * 8, 128), F32)),
        in_specs=[pl.BlockSpec(memory_space=pl.ANY)] * 7
        + [pl.BlockSpec(memory_space=pltpu.VMEM), pl.BlockSpec(memory_space=pltpu.SMEM), pl.BlockSpec(memory_space=pltpu.SMEM)],
        out_specs=[pl.BlockSpec(memory_space=pl.ANY)] * 2,
        scratch_shapes=[
            vmem((NL + 1) * LVL), vmem(NL * LVL), vmem(256), vmem(256), vmem(1024), vmem(480, 256, BF16), vmem(128, 256), vmem(2 * NBP, 3 * NBP, BF16),
            vmem(512), vmem(512), vmem(512), vmem(512), vmem(512), vmem(512), vmem(256), vmem(8),
            vmem(32), vmem(NG * 32), vmem(8), vmem(NG * 8), vmem((NG + 1) * 16), vmem((NG + 1) * 16),
            vmem(8), vmem(LVL), vmem(LVL), vmem(128), vmem(128), vmem(128), vmem(128), vmem(128), vmem(128), vmem(128),
            vmem(NBP * 8), vmem(LVL), vmem(8),
            dma((6,)), dma((8,)), dma((16,)), dma,
            dma((4, NP)), dma((4, NP)), dma((NG,)), dma((NG,)), dma((NG,)), dma((NG,)), dma((6,)), dma((6,)),
        ],
        compiler_params=pltpu.CompilerParams(collective_id=0, has_side_effects=True, vmem_limit_bytes=60 * 1024 * 1024),
        name="slab_step",
    )(
        bins.reshape(NL * LVL, 128), u.reshape(256, 128), w.reshape(256, 128), binv.reshape(1024, 128),
        jnp.asarray(mats), jnp.asarray(tw), coll, ids, fall, counts,
    )
    return out.reshape(NL, NB, 8, 128), pres.reshape(NL, 8, 128)


def solution(mesh):
    return jax.shard_map(
        body,
        mesh=mesh,
        in_specs=(
            P("gz", None, None, "gx"),
            P("gz", None, "gx"),
            P("gz", None, "gx"),
            P(),
            P(),
            P(),
            P("gz", "gx"),
            P("gz", "gx"),
            P("gz", None, "gx"),
        ),
        out_specs=(P("gz", None, None, "gx"), P("gz", None, "gx")),
        check_vma=False,
    )
```

```python
import functools
import math

import jax
import jax.numpy as jnp
import numpy as np
from jax import lax
from jax.experimental import pallas as pl
from jax.experimental.pallas import tpu as pltpu
from jax.sharding import PartitionSpec as P

F32 = jnp.float32
BF16 = jnp.bfloat16
MESH = pl.DeviceIdType.MESH
NB = 33
NBP = 48
NL = 32
NG = 8
NP = 32
LVL = NB * 8


def halves(x):
    hi = np.asarray(np.asarray(x, np.float32), jnp.bfloat16)
    lo = np.asarray(np.asarray(x - hi.astype(np.float64), np.float32), jnp.bfloat16)
    return hi, lo


def tables():
    p = np.arange(32)
    c = np.arange(128)
    pj = 2.0 * math.pi / 32 * (p[:, None] * c[None, :] % 32)
    cj = 2.0 * math.pi / 4096 * (c[:, None] * c[None, :])
    cos, sin = np.cos(pj), np.sin(pj)
    e_hi, e_lo = halves(np.concatenate([cos, -sin], 1))
    e3 = np.concatenate([e_hi, e_hi, e_lo], 0)
    fwd = np.concatenate([np.concatenate([cos, sin], 1), np.concatenate([-sin, cos], 1)], 0)
    f2 = np.concatenate(halves(fwd), 0)
    g = np.concatenate([np.concatenate([cos, sin], 1), np.concatenate([-sin, cos], 1)], 0)
    g_hi, g_lo = halves(g)
    g3 = np.concatenate([g_hi, g_hi, g_lo], 0)
    h2 = np.concatenate(halves(np.concatenate([cos, -sin], 1) / 4096.0), 0)
    mats = np.concatenate([e3, f2, g3, h2], 0)
    tw = np.concatenate([np.cos(cj), -np.sin(cj)], 1).astype(np.float32)
    return mats, tw


def split(x):
    hi = x.astype(BF16)
    lo = (x - hi.astype(F32)).astype(BF16)
    return hi, lo


def dot(a, b):
    return jnp.dot(a, b, preferred_element_type=F32)


def dot_t(a, b):
    return lax.dot_general(a, b, (((0,), (0,)), ((), ())), preferred_element_type=F32)


def kernel_body(
    bins_h, u_h, w_h, binv_h, mats_h, tw_h, kern_h, redi_h, ids_h, fall_h, cnt_h,
    out_v, pres_v,
    bins_v, u_v, w_v, binv_v, mats_v, tw_v, kern_v, redi_v, ids_v, fall_v, cnt_v, coll_v, fall_t,
    send1, x1, send2, x2, send3, x3, send4, wtop,
    esend, edges, csend, corners, bpad, tpad,
    wlow, zlo, zhi, send_f, send_l, send_u, halo_r, halo_l, halo_u, prior,
    adv, fz, mask_v,
    in_sem, bin_sem,
    a2a_send, a2a_recv, e_send, e_recv, c_send, c_recv, h_send, h_recv, w_send, w_recv,
):
    me = lax.axis_index("gx")
    g = lax.axis_index("gz")
    right = {"gx": lax.rem(me + 1, NP)}
    left = {"gx": lax.rem(me + NP - 1, NP)}
    above = {"gz": lax.rem(g + 1, NG)}
    below = {"gz": lax.rem(g + NG - 1, NG)}

    lane = lax.broadcasted_iota(jnp.int32, (8, 128), 1)
    sub = lax.broadcasted_iota(jnp.int32, (8, 128), 0)

    barrier = pltpu.get_barrier_semaphore()

    def peer_of(t):
        half = (t + 1) // 2
        odd = lax.rem(t, 2)
        o = 16 + odd * half - (1 - odd) * half
        return lax.rem(me + o, NP)

    def greet(gx, gz):
        pl.semaphore_signal(barrier, inc=1, device_id={"gx": gx, "gz": gz}, device_id_type=MESH)

    def greet_x(t, _):
        greet(peer_of(t), g)
        return 0

    def greet_z(o, _):
        greet(me, lax.rem(g + o, NG))
        return 0

    def greet_low(o, _):
        greet(o, lax.rem(g + NG - 1, NG))
        return 0

    not_first = g > 0
    not_last = g < NG - 1
    takes_w = (me == 0) & not_first
    lax.fori_loop(0, NP - 1, greet_x, 0)
    lax.fori_loop(1, NG, greet_z, 0)

    @pl.when(takes_w)
    def _():
        lax.fori_loop(1, NP, greet_low, 0)

    loads = [
        pltpu.make_async_copy(s, d, in_sem.at[i])
        for i, (s, d) in enumerate(
            [(u_h, u_v), (w_h, w_v), (binv_h, binv_v), (mats_h, mats_v), (tw_h, tw_v),
             (kern_h, kern_v), (redi_h, redi_v), (ids_h, ids_v), (fall_h, fall_v), (cnt_h, cnt_v)]
        )
    ]
    loads[0].start()
    loads[1].start()
    bin_loads = [
        pltpu.make_async_copy(bins_h.at[pl.ds(i * 4 * LVL, 4 * LVL)], bins_v.at[pl.ds(i * 4 * LVL, 4 * LVL)], bin_sem.at[i])
        for i in range(8)
    ]
    for i in range(8):
        bin_loads[i].start()
    for c in loads[2:]:
        c.start()
    loads[0].wait()
    loads[1].wait()

    def tile_div(q, w_under):
        u = u_v[pl.ds(q * 8, 8), :]
        before = jnp.where(lane == 0, 0.0, pltpu.roll(u, 1, 1))
        d = (u - before) + (w_v[pl.ds(q * 8, 8), :] - w_under)
        row = jnp.sum(jnp.where(lane == sub, jnp.broadcast_to(u[:, 127:128], (8, 128)), 0.0), axis=0, keepdims=True)
        send1[pl.ds(q * 16, 8), :] = d
        send1[pl.ds(q * 16 + 8, 8), :] = jnp.broadcast_to(row, (8, 128))

    tile_div(0, jnp.zeros((8, 128), F32))

    def div_step(q, _):
        tile_div(q, w_v[pl.ds(q * 8 - 8, 8), :])
        return 0

    lax.fori_loop(1, NL, div_step, 0)

    @pl.when(jnp.logical_not(takes_w))
    def _():
        wtop[...] = jnp.zeros((256, 128), F32)

    extra = jnp.where(not_last & (me != 0), 1, 0)
    pl.semaphore_wait(barrier, NP - 1 + NG - 1 + extra)

    def w_msg(p):
        return pltpu.make_async_remote_copy(
            src_ref=w_v.at[pl.ds(248, 8)], dst_ref=wtop.at[pl.ds(pl.multiple_of(p * 8, 8), 8)],
            send_sem=w_send, recv_sem=w_recv.at[p], device_id={"gx": me * 0, "gz": lax.rem(g + 1, NG)}, device_id_type=MESH)

    @pl.when(not_last)
    def _():
        w_msg(me).start()

    def msg(stage, src, dst, rows, peer, at):
        s0 = pl.multiple_of(peer * at, 8)
        d0 = pl.multiple_of(me * at, 8)
        return pltpu.make_async_remote_copy(
            src_ref=src.at[pl.ds(s0, rows)], dst_ref=dst.at[pl.ds(d0, rows)],
            send_sem=a2a_send.at[stage, peer], recv_sem=a2a_recv.at[stage, me],
            device_id={"gx": peer}, device_id_type=MESH)

    def send_all(stage, src, dst, rows, at):
        def step(t, _):
            msg(stage, src, dst, rows, peer_of(t), at).start()
            return 0
        lax.fori_loop(0, NP - 1, step, 0)

    def wait_all(stage, src, dst, rows, at):
        def step(t, _):
            peer = lax.rem(me + t + 1, NP)
            d0 = pl.multiple_of(peer * at, 8)
            pltpu.make_async_remote_copy(
                src_ref=src.at[pl.ds(d0, rows)], dst_ref=dst.at[pl.ds(d0, rows)],
                send_sem=a2a_send.at[stage, peer], recv_sem=a2a_recv.at[stage, peer],
                device_id={"gx": peer}, device_id_type=MESH).wait()
            return 0
        lax.fori_loop(0, NP - 1, step, 0)

    def own(src, dst, rows, at):
        m0 = pl.multiple_of(me * at, 8)
        dst[pl.ds(m0, rows), :] = src[pl.ds(m0, rows), :]

    send_all(0, send1, x1, 9, 16)
    own(send1, x1, 16, 16)

    bin_loads[7].wait()
    bin_loads[0].wait()
    z_up = pltpu.make_async_remote_copy(
        src_ref=bins_v.at[pl.ds(31 * LVL, LVL)], dst_ref=zlo, send_sem=h_send.at[1], recv_sem=h_recv.at[1],
        device_id=above, device_id_type=MESH)
    z_down = pltpu.make_async_remote_copy(
        src_ref=bins_v.at[pl.ds(0, LVL)], dst_ref=zhi, send_sem=h_send.at[2], recv_sem=h_recv.at[2],
        device_id=below, device_id_type=MESH)
    w_up = pltpu.make_async_remote_copy(
        src_ref=w_v.at[pl.ds(248, 8)], dst_ref=wlow, send_sem=h_send.at[0], recv_sem=h_recv.at[0],
        device_id=above, device_id_type=MESH)
    w_up.start()
    z_up.start()
    z_down.start()

    loads[2].wait()
    csend[...] = jnp.zeros((8, 128), F32)
    for i, r in enumerate((0, 31, 31 * 32, 31 * 32 + 31)):
        csend[pl.ds(i, 1), :] = binv_v[pl.ds(r, 1), :]

    def z_msg(src, dst, rows, peer, ss, rs):
        d0 = pl.multiple_of(g * rows, 8)
        return pltpu.make_async_remote_copy(
            src_ref=src, dst_ref=dst.at[pl.ds(d0, rows)], send_sem=ss.at[peer], recv_sem=rs.at[g],
            device_id={"gz": peer}, device_id_type=MESH)

    def send_z(src, dst, rows, ss, rs):
        def step(o, _):
            z_msg(src, dst, rows, lax.rem(g + o, NG), ss, rs).start()
            return 0
        lax.fori_loop(1, NG, step, 0)
        dst[pl.ds(pl.multiple_of(g * rows, 8), rows), :] = src[...]

    def wait_z(src, dst, rows, ss, rs):
        def step(o, _):
            peer = lax.rem(g + o, NG)
            pltpu.make_async_remote_copy(
                src_ref=src, dst_ref=dst.at[pl.ds(pl.multiple_of(peer * rows, 8), rows)], send_sem=ss.at[peer], recv_sem=rs.at[peer],
                device_id={"gz": peer}, device_id_type=MESH).wait()
            return 0
        lax.fori_loop(1, NG, step, 0)

    send_z(csend, corners, 8, c_send, c_recv)

    for i in range(1, 7):
        bin_loads[i].wait()

    def pack(i, _):
        first = jnp.zeros((8, 128), F32)
        last = jnp.zeros((8, 128), F32)
        for r in range(2):
            for m in range(NB):
                v = bins_v[pl.ds((2 * i + r) * LVL + m * 8, 8), :]
                hit = lane == (NB * r + m)
                first = jnp.where(hit, jnp.broadcast_to(v[:, 0:1], (8, 128)), first)
                last = jnp.where(hit, jnp.broadcast_to(v[:, 127:128], (8, 128)), last)
        speeds = jnp.where(
            lane < NB,
            jnp.broadcast_to(u_v[pl.ds(i * 16, 8), :][:, 127:128], (8, 128)),
            jnp.broadcast_to(u_v[pl.ds(i * 16 + 8, 8), :][:, 127:128], (8, 128)))
        send_f[pl.ds(i * 8, 8), :] = first
        send_l[pl.ds(i * 8, 8), :] = last
        send_u[pl.ds(i * 8, 8), :] = speeds
        return 0

    lax.fori_loop(0, NL // 2, pack, 0)
    x_copies = [
        pltpu.make_async_remote_copy(src_ref=s, dst_ref=d, send_sem=h_send.at[i], recv_sem=h_recv.at[i], device_id=to, device_id_type=MESH)
        for i, s, d, to in ((3, send_f, halo_r, left), (4, send_l, halo_l, right), (5, send_u, halo_u, right))
    ]
    for c in x_copies:
        c.start()

    for c in loads[3:]:
        c.wait()

    block = lax.broadcasted_iota(jnp.int32, (64, 64), 0)
    slot = lax.broadcasted_iota(jnp.int32, (64, 64), 1)
    hits = (jnp.broadcast_to(ids_v[...], (64, 64)) == block) & (slot < jnp.broadcast_to(cnt_v[...], (64, 64)))
    marks = jnp.max(jnp.where(hits, 1.0, 0.0), axis=1, keepdims=True)
    col_block = lax.broadcasted_iota(jnp.int32, (16, 128), 1) // 8
    row_block = lax.broadcasted_iota(jnp.int32, (16, 128), 0)
    for bz in range(4):
        wide = jnp.broadcast_to(marks[bz * 16:bz * 16 + 16, :], (16, 128))
        mask_v[pl.ds(bz, 1), :] = jnp.sum(jnp.where(col_block == row_block, wide, 0.0), axis=0, keepdims=True)

    adv[...] = jnp.zeros((NBP * 8, 128), F32)
    coll_v[...] = jnp.zeros((2 * NBP, 3 * NBP), F32)
    pos = lax.broadcasted_iota(jnp.int32, (NB, 3 * NBP), 1)
    row = lax.broadcasted_iota(jnp.int32, (NB, 3 * NBP), 0)
    pick_hi = jnp.where((pos == row) | (pos == row + 2 * NBP), 1.0, 0.0).astype(BF16)
    pick_lo = jnp.where(pos == row + NBP, 1.0, 0.0).astype(BF16)
    for n, ref in enumerate((kern_v, redi_v)):
        hi, lo = split(ref[...])
        coll_v[pl.ds(n * NBP, NB), :] = dot_t(hi, pick_hi) + dot_t(lo, pick_lo)
    for m in range(NB):
        fall_t[pl.ds(m * 8, 8), :] = jnp.broadcast_to(fall_v[:, m:m + 1], (8, 128))

    def level(z, i, r):
        u = u_v[pl.ds(z * 8, 8), :]
        u_pos, u_neg = jnp.maximum(u, 0.0), jnp.minimum(u, 0.0)
        w = w_v[pl.ds(z * 8, 8), :]
        hr = halo_r[pl.ds(i * 8, 8), :]
        pf = prior[pl.ds(i * 8, 8), :]
        base = z * LVL
        for m in range(NB):
            k = NB * r + m
            b = bins_v[pl.ds(base + m * 8, 8), :]
            up = bins_v[pl.ds(base + LVL + m * 8, 8), :]
            nxt = jnp.where(lane == 127, jnp.broadcast_to(hr[:, k:k + 1], (8, 128)), pltpu.roll(b, 127, 1))
            flux = u_pos * b + u_neg * nxt
            prev = jnp.where(lane == 0, jnp.broadcast_to(pf[:, k:k + 1], (8, 128)), pltpu.roll(flux, 1, 1))
            c = w - fall_t[pl.ds(m * 8, 8), :]
            top = jnp.maximum(c, 0.0) * b + jnp.minimum(c, 0.0) * up
            s = pl.ds(m * 8, 8)
            adv[s, :] = b - (flux - prev) - (top - fz[s, :])
            fz[s, :] = top
        mark = jnp.broadcast_to(mask_v[pl.ds(z // 8, 1), :], (NBP, 128))
        grow_w = coll_v[pl.ds(0, NBP), :].astype(BF16)
        redi_w = coll_v[pl.ds(NBP, NBP), :].astype(BF16)
        for h in range(4):
            ys = (2 * h, 2 * h + 1)
            v = jnp.concatenate([adv[pl.ds(y, NBP, stride=8), :] for y in ys], axis=1)
            hi, lo = split(v)
            rate = dot(grow_w, jnp.concatenate([hi, hi, lo], axis=0))
            hi, lo = split(v * rate)
            tend = dot(redi_w, jnp.concatenate([hi, hi, lo], axis=0))
            for n, y in enumerate(ys):
                part = slice(128 * n, 128 * n + 128)
                new = v[:, part] + tend[:, part] * mark
                out_v[pl.ds(base + y, NB, stride=8), :] = new[:NB]

    def levels(first, last):
        def step(i, _):
            level(2 * i, i, 0)
            level(2 * i + 1, i, 1)
            return 0
        lax.fori_loop(first, last, step, 0)

    wait_all(0, send1, x1, 9, 16)

    @pl.when(takes_w)
    def _():
        def step(p, _):
            w_msg(p).wait_recv()
            return 0
        lax.fori_loop(0, NP, step, 0)

    borders = x1[pl.ds(8, NP, stride=16), :]
    borders = pltpu.roll(borders, 1, 0)
    lane32 = lax.broadcasted_iota(jnp.int32, (32, 128), 1)
    e3 = mats_v[pl.ds(0, 96), :]
    f2 = mats_v[pl.ds(96, 128), :]
    twr = tw_v[:, 0:128]
    twi = tw_v[:, 128:256]
    for h in range(4):
        us = []
        for y in (2 * h, 2 * h + 1):
            xy = x1[pl.ds(y, NP, stride=16), :] - wtop[pl.ds(y, NP, stride=8), :]
            shifted = borders if y == 0 else pltpu.roll(borders, 128 - y, 1)
            xy = xy - jnp.where(lane32 == 0, shifted, 0.0)
            hi, lo = split(xy)
            yy = dot_t(jnp.concatenate([hi, lo, hi], axis=0), e3)
            yr, yi = yy[:, :128], yy[:, 128:]
            us.append(jnp.concatenate([yr * twr - yi * twi, yr * twi + yi * twr], axis=0))
        hi, lo = split(jnp.concatenate(us, axis=1))
        both = dot(f2, hi)
        spec = both[:64] + both[64:] + dot(f2[:64], lo)
        for n, y in enumerate((2 * h, 2 * h + 1)):
            part = slice(128 * n, 128 * n + 128)
            send2[pl.ds(y, NP, stride=16), :] = spec[:32, part]
            send2[pl.ds(8 + y, NP, stride=16), :] = spec[32:, part]
    send_all(1, send2, x2, 16, 16)
    own(send2, x2, 16, 16)

    z_up.wait()
    w_up.wait()
    z_down.wait()
    for c in x_copies:
        c.wait()

    def prior_step(i, _):
        s = pl.ds(i * 8, 8)
        speed = halo_u[s, :]
        prior[s, :] = jnp.maximum(speed, 0.0) * halo_l[s, :] + jnp.minimum(speed, 0.0) * send_f[s, :]
        return 0

    lax.fori_loop(0, NL // 2, prior_step, 0)

    w_low = jnp.where(not_first, wlow[...], 0.0)

    def low_face(m, _):
        s = pl.ds(m * 8, 8)
        c = w_low - fall_t[s, :]
        fz[s, :] = jnp.maximum(c, 0.0) * jnp.where(not_first, zlo[s, :], 0.0) + jnp.minimum(c, 0.0) * bins_v[s, :]
        bins_v[pl.ds(NL * LVL + m * 8, 8), :] = jnp.where(not_last, zhi[s, :], 0.0)
        return 0

    lax.fori_loop(0, NB, low_face, 0)


    levels(0, CUT[0])

    wait_all(1, send2, x2, 16, 16)

    def apply_rows(rows):
        accs = [None] * len(rows)
        for j in range(NL):
            s = x2[pl.ds(j * 16, 16), :]
            for n, i in enumerate(rows):
                b = jnp.broadcast_to(binv_v[pl.ds(i * 32 + j, 1), :], (16, 128))
                accs[n] = b * s if accs[n] is None else accs[n] + b * s
        return accs

    low, high = apply_rows((0, 31))
    esend[pl.ds(0, 16), :] = low
    esend[pl.ds(16, 16), :] = high
    send_z(esend, edges, 32, e_send, e_recv)

    def solve_step(t, _):
        rows = [t * 4 + n for n in range(4)]
        for i, acc in zip(rows, apply_rows(rows)):
            send3[pl.ds(i * 16, 16), :] = acc
        return 0

    lax.fori_loop(0, NL // 4, solve_step, 0)
    levels(CUT[0], CUT[1])
    wait_z(csend, corners, 8, c_send, c_recv)
    wait_z(esend, edges, 32, e_send, e_recv)

    zero = jnp.zeros((16, 128), F32)
    e0 = [edges[pl.ds(k * 32, 16), :] for k in range(NG)]
    e1 = [edges[pl.ds(k * 32 + 16, 16), :] for k in range(NG)]

    def corner(k, i):
        return jnp.broadcast_to(corners[pl.ds(k * 8 + i, 1), :], (16, 128))

    bs, ts = e0, e1
    for _ in range(2):
        nb, nt = [], []
        for k in range(NG):
            over = bs[k + 1] if k < NG - 1 else zero
            under = ts[k - 1] if k > 0 else zero
            nb.append(e0[k] + corner(k, 1) * over + corner(k, 0) * under)
            nt.append(e1[k] + corner(k, 3) * over + corner(k, 2) * under)
        bs, ts = nb, nt
    for k in range(NG):
        bpad[pl.ds(k * 16, 16), :] = bs[k]
        tpad[pl.ds(k * 16 + 16, 16), :] = ts[k]
    bpad[pl.ds(NG * 16, 16), :] = zero
    tpad[pl.ds(0, 16), :] = zero
    over = bpad[pl.ds(pl.multiple_of(g * 16 + 16, 8), 16), :]
    under = tpad[pl.ds(pl.multiple_of(g * 16, 8), 16), :]

    def update(i, _):
        s = pl.ds(i * 16, 16)
        top = jnp.broadcast_to(binv_v[pl.ds(i * 32 + 31, 1), :], (16, 128))
        bot = jnp.broadcast_to(binv_v[pl.ds(i * 32, 1), :], (16, 128))
        send3[s, :] = send3[s, :] + top * over + bot * under
        return 0

    lax.fori_loop(0, NL, update, 0)
    send_all(2, send3, x3, 16, 16)
    own(send3, x3, 16, 16)

    levels(CUT[1], CUT[2])

    wait_all(2, send3, x3, 16, 16)
    g3 = mats_v[pl.ds(224, 192), :]
    h2 = mats_v[pl.ds(416, 64), :]
    for h in range(4):
        zs = []
        for y in (2 * h, 2 * h + 1):
            s2 = jnp.concatenate([x3[pl.ds(y, NP, stride=16), :], x3[pl.ds(8 + y, NP, stride=16), :]], axis=0)
            hi, lo = split(s2)
            vv = dot_t(jnp.concatenate([hi, lo, hi], axis=0), g3)
            vr, vi = vv[:, :128], vv[:, 128:]
            zs.append(jnp.concatenate([vr * twr + vi * twi, vi * twr - vr * twi], axis=0))
        hi, lo = split(jnp.concatenate(zs, axis=1))
        both = dot(h2, hi)
        pr = both[:32] + both[32:] + dot(h2[:32], lo)
        for n, y in enumerate((2 * h, 2 * h + 1)):
            send4[pl.ds(y, NP, stride=8), :] = pr[:, 128 * n:128 * n + 128]
    send_all(3, send4, pres_v, 8, 8)
    own(send4, pres_v, 8, 8)

    levels(CUT[2], NL // 2)

    @pl.when(not_last)
    def _():
        w_msg(me).wait_send()

    wait_all(3, send4, pres_v, 8, 8)


def write_body(out_v, pres_v, out_h, pres_h, sem):
    copies = [pltpu.make_async_copy(pres_v, pres_h, sem.at[8])]
    for i in range(8):
        s = pl.ds(i * 4 * LVL, 4 * LVL)
        copies.append(pltpu.make_async_copy(out_v.at[s], out_h.at[s], sem.at[i]))
    for c in copies:
        c.start()
    for c in copies:
        c.wait()


CUT = (6, 8, 14)


def body(bins, u, w, fall, kern, redi, ids, counts, binv):
    mats, tw = tables()
    vmem = lambda rows, cols=128, t=F32: pltpu.VMEM((rows, cols), t)
    dma = pltpu.SemaphoreType.DMA
    out, pres = pl.pallas_call(
        kernel_body,
        out_shape=(pltpu.VMEM((NL * LVL, 128), F32), pltpu.VMEM((NL * 8, 128), F32)),
        in_specs=[pl.BlockSpec(memory_space=pl.ANY)] * 11,
        out_specs=[pl.BlockSpec(memory_space=pltpu.VMEM)] * 2,
        scratch_shapes=[
            vmem((NL + 1) * LVL), vmem(256), vmem(256), vmem(1024), vmem(480, 256, BF16), vmem(128, 256),
            vmem(NB, NB), vmem(NB, NB), vmem(1, 64, jnp.int32), vmem(1, NB), vmem(1, 1, jnp.int32), vmem(2 * NBP, 3 * NBP), vmem(LVL),
            vmem(512), vmem(512), vmem(512), vmem(512), vmem(512), vmem(512), vmem(256), vmem(256),
            vmem(32), vmem(NG * 32), vmem(8), vmem(NG * 8), vmem((NG + 1) * 16), vmem((NG + 1) * 16),
            vmem(8), vmem(LVL), vmem(LVL), vmem(128), vmem(128), vmem(128), vmem(128), vmem(128), vmem(128), vmem(128),
            vmem(NBP * 8), vmem(LVL), vmem(8),
            dma((10,)), dma((8,)),
            dma((4, NP)), dma((4, NP)), dma((NG,)), dma((NG,)), dma((NG,)), dma((NG,)), dma((6,)), dma((6,)), dma, dma((NP,)),
        ],
        compiler_params=pltpu.CompilerParams(collective_id=0, has_side_effects=True, vmem_limit_bytes=24 * 1024 * 1024),
        name="slab_step",
    )(
        bins.reshape(NL * LVL, 128), u.reshape(256, 128), w.reshape(256, 128), binv.reshape(1024, 128),
        jnp.asarray(mats), jnp.asarray(tw), kern, redi, ids, fall.reshape(1, NB), counts,
    )
    out, pres = pl.pallas_call(
        write_body,
        out_shape=(jax.ShapeDtypeStruct((NL * LVL, 128), F32), jax.ShapeDtypeStruct((NL * 8, 128), F32)),
        in_specs=[pl.BlockSpec(memory_space=pltpu.VMEM)] * 2,
        out_specs=[pl.BlockSpec(memory_space=pl.ANY)] * 2,
        scratch_shapes=[dma((9,))],
        compiler_params=pltpu.CompilerParams(vmem_limit_bytes=1024 * 1024),
        name="write_out",
    )(out, pres)
    return out.reshape(NL, NB, 8, 128), pres.reshape(NL, 8, 128)


def solution(mesh):
    return jax.shard_map(
        body,
        mesh=mesh,
        in_specs=(
            P("gz", None, None, "gx"),
            P("gz", None, "gx"),
            P("gz", None, "gx"),
            P(),
            P(),
            P(),
            P("gz", "gx"),
            P("gz", "gx"),
            P("gz", None, "gx"),
        ),
        out_specs=(P("gz", None, None, "gx"), P("gz", None, "gx")),
        check_vma=False,
    )
```

```python
import functools
import math

import jax
import jax.numpy as jnp
import numpy as np
from jax import lax
from jax.experimental import pallas as pl
from jax.experimental.pallas import tpu as pltpu
from jax.sharding import PartitionSpec as P

F32 = jnp.float32
BF16 = jnp.bfloat16
MESH = pl.DeviceIdType.MESH
NB = 33
NBP = 48
NL = 32
NG = 8
NP = 32
LVL = NB * 8


def halves(x):
    hi = np.asarray(np.asarray(x, np.float32), jnp.bfloat16)
    lo = np.asarray(np.asarray(x - hi.astype(np.float64), np.float32), jnp.bfloat16)
    return hi, lo


def tables():
    p = np.arange(32)
    c = np.arange(128)
    pj = 2.0 * math.pi / 32 * (p[:, None] * c[None, :] % 32)
    cj = 2.0 * math.pi / 4096 * (c[:, None] * c[None, :])
    cos, sin = np.cos(pj), np.sin(pj)
    e_hi, e_lo = halves(np.concatenate([cos, -sin], 1))
    e3 = np.concatenate([e_hi, e_hi, e_lo], 0)
    fwd = np.concatenate([np.concatenate([cos, sin], 1), np.concatenate([-sin, cos], 1)], 0)
    f2 = np.concatenate(halves(fwd), 0)
    g = np.concatenate([np.concatenate([cos, sin], 1), np.concatenate([-sin, cos], 1)], 0)
    g_hi, g_lo = halves(g)
    g3 = np.concatenate([g_hi, g_hi, g_lo], 0)
    h2 = np.concatenate(halves(np.concatenate([cos, -sin], 1) / 4096.0), 0)
    mats = np.concatenate([e3, f2, g3, h2], 0)
    tw = np.concatenate([np.cos(cj), -np.sin(cj)], 1).astype(np.float32)
    return mats, tw


def split(x):
    hi = x.astype(BF16)
    lo = (x - hi.astype(F32)).astype(BF16)
    return hi, lo


def dot(a, b):
    return jnp.dot(a, b, preferred_element_type=F32)


def dot_t(a, b):
    return lax.dot_general(a, b, (((0,), (0,)), ((), ())), preferred_element_type=F32)


def kernel_body(
    bins_h, u_h, w_h, binv_h, mats_h, tw_h, kern_h, redi_h, ids_h, fall_h, cnt_h,
    out_v, pres_v,
    bins_v, u_v, w_v, binv_v, mats_v, tw_v, kern_v, redi_v, ids_v, fall_v, cnt_v, coll_v, fall_t,
    send1, x1, send2, x2, send3, x3, send4, wtop,
    esend, edges, csend, corners, bpad, tpad,
    wlow, zlo, zhi, send_f, send_l, send_u, halo_r, halo_l, halo_u, prior,
    adv, fz, mask_v,
    in_sem, bin_sem,
    a2a_send, a2a_recv, e_send, e_recv, c_send, c_recv, h_send, h_recv, w_send, w_recv,
):
    me = lax.axis_index("gx")
    g = lax.axis_index("gz")
    right = {"gx": lax.rem(me + 1, NP)}
    left = {"gx": lax.rem(me + NP - 1, NP)}
    above = {"gz": lax.rem(g + 1, NG)}
    below = {"gz": lax.rem(g + NG - 1, NG)}

    lane = lax.broadcasted_iota(jnp.int32, (8, 128), 1)
    sub = lax.broadcasted_iota(jnp.int32, (8, 128), 0)

    barrier = pltpu.get_barrier_semaphore()

    def peer_of(t):
        half = (t + 1) // 2
        odd = lax.rem(t, 2)
        o = 16 + odd * half - (1 - odd) * half
        return lax.rem(me + o, NP)

    def greet(gx, gz):
        pl.semaphore_signal(barrier, inc=1, device_id={"gx": gx, "gz": gz}, device_id_type=MESH)

    def greet_x(t, _):
        greet(peer_of(t), g)
        return 0

    def greet_z(o, _):
        greet(me, lax.rem(g + o, NG))
        return 0

    def greet_low(o, _):
        greet(o, lax.rem(g + NG - 1, NG))
        return 0

    not_first = g > 0
    not_last = g < NG - 1
    takes_w = (me == 0) & not_first
    lax.fori_loop(0, NP - 1, greet_x, 0)
    lax.fori_loop(1, NG, greet_z, 0)

    @pl.when(takes_w)
    def _():
        lax.fori_loop(1, NP, greet_low, 0)

    loads = [
        pltpu.make_async_copy(s, d, in_sem.at[i])
        for i, (s, d) in enumerate(
            [(u_h, u_v), (w_h, w_v), (binv_h, binv_v), (mats_h, mats_v), (tw_h, tw_v),
             (kern_h, kern_v), (redi_h, redi_v), (ids_h, ids_v), (fall_h, fall_v), (cnt_h, cnt_v)]
        )
    ]
    loads[0].start()
    loads[1].start()
    bin_loads = [
        pltpu.make_async_copy(bins_h.at[pl.ds(i * 4 * LVL, 4 * LVL)], bins_v.at[pl.ds(i * 4 * LVL, 4 * LVL)], bin_sem.at[i])
        for i in range(8)
    ]
    for i in range(8):
        bin_loads[i].start()
    for c in loads[2:]:
        c.start()
    loads[0].wait()
    loads[1].wait()

    def tile_div(q, w_under):
        u = u_v[pl.ds(q * 8, 8), :]
        before = jnp.where(lane == 0, 0.0, pltpu.roll(u, 1, 1))
        d = (u - before) + (w_v[pl.ds(q * 8, 8), :] - w_under)
        row = jnp.sum(jnp.where(lane == sub, jnp.broadcast_to(u[:, 127:128], (8, 128)), 0.0), axis=0, keepdims=True)
        send1[pl.ds(q * 16, 8), :] = d
        send1[pl.ds(q * 16 + 8, 8), :] = jnp.broadcast_to(row, (8, 128))

    tile_div(0, jnp.zeros((8, 128), F32))

    def div_step(q, _):
        tile_div(q, w_v[pl.ds(q * 8 - 8, 8), :])
        return 0

    lax.fori_loop(1, NL, div_step, 0)

    @pl.when(jnp.logical_not(takes_w))
    def _():
        wtop[...] = jnp.zeros((256, 128), F32)

    extra = jnp.where(not_last & (me != 0), 1, 0)
    pl.semaphore_wait(barrier, NP - 1 + NG - 1 + extra)

    def w_msg(p):
        return pltpu.make_async_remote_copy(
            src_ref=w_v.at[pl.ds(248, 8)], dst_ref=wtop.at[pl.ds(pl.multiple_of(p * 8, 8), 8)],
            send_sem=w_send, recv_sem=w_recv.at[p], device_id={"gx": me * 0, "gz": lax.rem(g + 1, NG)}, device_id_type=MESH)

    @pl.when(not_last)
    def _():
        w_msg(me).start()

    def msg(stage, src, dst, rows, peer, at):
        s0 = pl.multiple_of(peer * at, 8)
        d0 = pl.multiple_of(me * at, 8)
        return pltpu.make_async_remote_copy(
            src_ref=src.at[pl.ds(s0, rows)], dst_ref=dst.at[pl.ds(d0, rows)],
            send_sem=a2a_send.at[stage, peer], recv_sem=a2a_recv.at[stage, me],
            device_id={"gx": peer}, device_id_type=MESH)

    def send_all(stage, src, dst, rows, at):
        def step(t, _):
            msg(stage, src, dst, rows, peer_of(t), at).start()
            return 0
        lax.fori_loop(0, NP - 1, step, 0)

    def wait_all(stage, src, dst, rows, at):
        def step(t, _):
            peer = lax.rem(me + t + 1, NP)
            d0 = pl.multiple_of(peer * at, 8)
            pltpu.make_async_remote_copy(
                src_ref=src.at[pl.ds(d0, rows)], dst_ref=dst.at[pl.ds(d0, rows)],
                send_sem=a2a_send.at[stage, peer], recv_sem=a2a_recv.at[stage, peer],
                device_id={"gx": peer}, device_id_type=MESH).wait()
            return 0
        lax.fori_loop(0, NP - 1, step, 0)

    def own(src, dst, rows, at):
        m0 = pl.multiple_of(me * at, 8)
        dst[pl.ds(m0, rows), :] = src[pl.ds(m0, rows), :]

    send_all(0, send1, x1, 9, 16)
    own(send1, x1, 16, 16)

    bin_loads[7].wait()
    bin_loads[0].wait()
    z_up = pltpu.make_async_remote_copy(
        src_ref=bins_v.at[pl.ds(31 * LVL, LVL)], dst_ref=zlo, send_sem=h_send.at[1], recv_sem=h_recv.at[1],
        device_id=above, device_id_type=MESH)
    z_down = pltpu.make_async_remote_copy(
        src_ref=bins_v.at[pl.ds(0, LVL)], dst_ref=zhi, send_sem=h_send.at[2], recv_sem=h_recv.at[2],
        device_id=below, device_id_type=MESH)
    w_up = pltpu.make_async_remote_copy(
        src_ref=w_v.at[pl.ds(248, 8)], dst_ref=wlow, send_sem=h_send.at[0], recv_sem=h_recv.at[0],
        device_id=above, device_id_type=MESH)
    w_up.start()
    z_up.start()
    z_down.start()

    loads[2].wait()
    csend[...] = jnp.zeros((8, 128), F32)
    for i, r in enumerate((0, 31, 31 * 32, 31 * 32 + 31)):
        csend[pl.ds(i, 1), :] = binv_v[pl.ds(r, 1), :]

    def z_msg(src, dst, rows, peer, ss, rs):
        d0 = pl.multiple_of(g * rows, 8)
        return pltpu.make_async_remote_copy(
            src_ref=src, dst_ref=dst.at[pl.ds(d0, rows)], send_sem=ss.at[peer], recv_sem=rs.at[g],
            device_id={"gz": peer}, device_id_type=MESH)

    def send_z(src, dst, rows, ss, rs):
        def step(o, _):
            z_msg(src, dst, rows, lax.rem(g + o, NG), ss, rs).start()
            return 0
        lax.fori_loop(1, NG, step, 0)
        dst[pl.ds(pl.multiple_of(g * rows, 8), rows), :] = src[...]

    def wait_z(src, dst, rows, ss, rs):
        def step(o, _):
            peer = lax.rem(g + o, NG)
            pltpu.make_async_remote_copy(
                src_ref=src, dst_ref=dst.at[pl.ds(pl.multiple_of(peer * rows, 8), rows)], send_sem=ss.at[peer], recv_sem=rs.at[peer],
                device_id={"gz": peer}, device_id_type=MESH).wait()
            return 0
        lax.fori_loop(1, NG, step, 0)

    send_z(csend, corners, 8, c_send, c_recv)

    for i in range(1, 7):
        bin_loads[i].wait()

    def pack(i, _):
        first = jnp.zeros((8, 128), F32)
        last = jnp.zeros((8, 128), F32)
        for r in range(2):
            for m in range(NB):
                v = bins_v[pl.ds((2 * i + r) * LVL + m * 8, 8), :]
                hit = lane == (NB * r + m)
                first = jnp.where(hit, jnp.broadcast_to(v[:, 0:1], (8, 128)), first)
                last = jnp.where(hit, jnp.broadcast_to(v[:, 127:128], (8, 128)), last)
        speeds = jnp.where(
            lane < NB,
            jnp.broadcast_to(u_v[pl.ds(i * 16, 8), :][:, 127:128], (8, 128)),
            jnp.broadcast_to(u_v[pl.ds(i * 16 + 8, 8), :][:, 127:128], (8, 128)))
        send_f[pl.ds(i * 8, 8), :] = first
        send_l[pl.ds(i * 8, 8), :] = last
        send_u[pl.ds(i * 8, 8), :] = speeds
        return 0

    lax.fori_loop(0, NL // 2, pack, 0)
    x_copies = [
        pltpu.make_async_remote_copy(src_ref=s, dst_ref=d, send_sem=h_send.at[i], recv_sem=h_recv.at[i], device_id=to, device_id_type=MESH)
        for i, s, d, to in ((3, send_f, halo_r, left), (4, send_l, halo_l, right), (5, send_u, halo_u, right))
    ]
    for c in x_copies:
        c.start()

    for c in loads[3:]:
        c.wait()

    block = lax.broadcasted_iota(jnp.int32, (64, 64), 0)
    slot = lax.broadcasted_iota(jnp.int32, (64, 64), 1)
    hits = (jnp.broadcast_to(ids_v[...], (64, 64)) == block) & (slot < jnp.broadcast_to(cnt_v[...], (64, 64)))
    marks = jnp.max(jnp.where(hits, 1.0, 0.0), axis=1, keepdims=True)
    col_block = lax.broadcasted_iota(jnp.int32, (16, 128), 1) // 8
    row_block = lax.broadcasted_iota(jnp.int32, (16, 128), 0)
    for bz in range(4):
        wide = jnp.broadcast_to(marks[bz * 16:bz * 16 + 16, :], (16, 128))
        mask_v[pl.ds(bz, 1), :] = jnp.sum(jnp.where(col_block == row_block, wide, 0.0), axis=0, keepdims=True)

    adv[...] = jnp.zeros((NBP * 8, 128), F32)
    coll_v[...] = jnp.zeros((2 * NBP, 3 * NBP), F32)
    pos = lax.broadcasted_iota(jnp.int32, (NB, 3 * NBP), 1)
    row = lax.broadcasted_iota(jnp.int32, (NB, 3 * NBP), 0)
    pick_hi = jnp.where((pos == row) | (pos == row + 2 * NBP), 1.0, 0.0).astype(BF16)
    pick_lo = jnp.where(pos == row + NBP, 1.0, 0.0).astype(BF16)
    for n, ref in enumerate((kern_v, redi_v)):
        hi, lo = split(ref[...])
        coll_v[pl.ds(n * NBP, NB), :] = dot_t(hi, pick_hi) + dot_t(lo, pick_lo)
    for m in range(NB):
        fall_t[pl.ds(m * 8, 8), :] = jnp.broadcast_to(fall_v[:, m:m + 1], (8, 128))

    def level(z, i, r):
        u = u_v[pl.ds(z * 8, 8), :]
        u_pos, u_neg = jnp.maximum(u, 0.0), jnp.minimum(u, 0.0)
        w = w_v[pl.ds(z * 8, 8), :]
        hr = halo_r[pl.ds(i * 8, 8), :]
        pf = prior[pl.ds(i * 8, 8), :]
        base = z * LVL
        for m in range(NB):
            k = NB * r + m
            b = bins_v[pl.ds(base + m * 8, 8), :]
            up = bins_v[pl.ds(base + LVL + m * 8, 8), :]
            nxt = jnp.where(lane == 127, jnp.broadcast_to(hr[:, k:k + 1], (8, 128)), pltpu.roll(b, 127, 1))
            flux = u_pos * b + u_neg * nxt
            prev = jnp.where(lane == 0, jnp.broadcast_to(pf[:, k:k + 1], (8, 128)), pltpu.roll(flux, 1, 1))
            c = w - fall_t[pl.ds(m * 8, 8), :]
            top = jnp.maximum(c, 0.0) * b + jnp.minimum(c, 0.0) * up
            s = pl.ds(m * 8, 8)
            adv[s, :] = b - (flux - prev) - (top - fz[s, :])
            fz[s, :] = top
        mark = jnp.broadcast_to(mask_v[pl.ds(z // 8, 1), :], (NBP, 128))
        grow_w = coll_v[pl.ds(0, NBP), :].astype(BF16)
        redi_w = coll_v[pl.ds(NBP, NBP), :].astype(BF16)
        for h in range(4):
            ys = (2 * h, 2 * h + 1)
            v = jnp.concatenate([adv[pl.ds(y, NBP, stride=8), :] for y in ys], axis=1)
            hi, lo = split(v)
            rate = dot(grow_w, jnp.concatenate([hi, hi, lo], axis=0))
            hi, lo = split(v * rate)
            tend = dot(redi_w, jnp.concatenate([hi, hi, lo], axis=0))
            for n, y in enumerate(ys):
                part = slice(128 * n, 128 * n + 128)
                new = v[:, part] + tend[:, part] * mark
                out_v[pl.ds(base + y, NB, stride=8), :] = new[:NB]

    def levels(first, last):
        def step(i, _):
            level(2 * i, i, 0)
            level(2 * i + 1, i, 1)
            return 0
        lax.fori_loop(first, last, step, 0)

    wait_all(0, send1, x1, 9, 16)

    @pl.when(takes_w)
    def _():
        def step(p, _):
            w_msg(p).wait_recv()
            return 0
        lax.fori_loop(0, NP, step, 0)

    borders = x1[pl.ds(8, NP, stride=16), :]
    borders = pltpu.roll(borders, 1, 0)
    lane32 = lax.broadcasted_iota(jnp.int32, (32, 128), 1)
    e3 = mats_v[pl.ds(0, 96), :]
    f2 = mats_v[pl.ds(96, 128), :]
    twr = tw_v[:, 0:128]
    twi = tw_v[:, 128:256]
    for h in range(4):
        us = []
        for y in (2 * h, 2 * h + 1):
            xy = x1[pl.ds(y, NP, stride=16), :] - wtop[pl.ds(y, NP, stride=8), :]
            shifted = borders if y == 0 else pltpu.roll(borders, 128 - y, 1)
            xy = xy - jnp.where(lane32 == 0, shifted, 0.0)
            hi, lo = split(xy)
            yy = dot_t(jnp.concatenate([hi, lo, hi], axis=0), e3)
            yr, yi = yy[:, :128], yy[:, 128:]
            us.append(jnp.concatenate([yr * twr - yi * twi, yr * twi + yi * twr], axis=0))
        hi, lo = split(jnp.concatenate(us, axis=1))
        both = dot(f2, hi)
        spec = both[:64] + both[64:] + dot(f2[:64], lo)
        for n, y in enumerate((2 * h, 2 * h + 1)):
            part = slice(128 * n, 128 * n + 128)
            send2[pl.ds(y, NP, stride=16), :] = spec[:32, part]
            send2[pl.ds(8 + y, NP, stride=16), :] = spec[32:, part]
    send_all(1, send2, x2, 16, 16)
    own(send2, x2, 16, 16)

    z_up.wait()
    w_up.wait()
    z_down.wait()
    for c in x_copies:
        c.wait()

    def prior_step(i, _):
        s = pl.ds(i * 8, 8)
        speed = halo_u[s, :]
        prior[s, :] = jnp.maximum(speed, 0.0) * halo_l[s, :] + jnp.minimum(speed, 0.0) * send_f[s, :]
        return 0

    lax.fori_loop(0, NL // 2, prior_step, 0)

    w_low = jnp.where(not_first, wlow[...], 0.0)

    def low_face(m, _):
        s = pl.ds(m * 8, 8)
        c = w_low - fall_t[s, :]
        fz[s, :] = jnp.maximum(c, 0.0) * jnp.where(not_first, zlo[s, :], 0.0) + jnp.minimum(c, 0.0) * bins_v[s, :]
        bins_v[pl.ds(NL * LVL + m * 8, 8), :] = jnp.where(not_last, zhi[s, :], 0.0)
        return 0

    lax.fori_loop(0, NB, low_face, 0)


    levels(0, CUT[0])

    wait_all(1, send2, x2, 16, 16)

    def apply_rows(rows):
        accs = [None] * len(rows)
        for j in range(NL):
            s = x2[pl.ds(j * 16, 16), :]
            for n, i in enumerate(rows):
                b = jnp.broadcast_to(binv_v[pl.ds(i * 32 + j, 1), :], (16, 128))
                accs[n] = b * s if accs[n] is None else accs[n] + b * s
        return accs

    low, high = apply_rows((0, 31))
    esend[pl.ds(0, 16), :] = low
    esend[pl.ds(16, 16), :] = high
    send_z(esend, edges, 32, e_send, e_recv)

    def solve_step(t, _):
        rows = [t * 4 + n for n in range(4)]
        for i, acc in zip(rows, apply_rows(rows)):
            send3[pl.ds(i * 16, 16), :] = acc
        return 0

    lax.fori_loop(0, NL // 4, solve_step, 0)
    levels(CUT[0], CUT[1])
    wait_z(csend, corners, 8, c_send, c_recv)
    wait_z(esend, edges, 32, e_send, e_recv)

    zero = jnp.zeros((16, 128), F32)
    e0 = [edges[pl.ds(k * 32, 16), :] for k in range(NG)]
    e1 = [edges[pl.ds(k * 32 + 16, 16), :] for k in range(NG)]

    def corner(k, i):
        return jnp.broadcast_to(corners[pl.ds(k * 8 + i, 1), :], (16, 128))

    bs, ts = e0, e1
    for _ in range(2):
        nb, nt = [], []
        for k in range(NG):
            over = bs[k + 1] if k < NG - 1 else zero
            under = ts[k - 1] if k > 0 else zero
            nb.append(e0[k] + corner(k, 1) * over + corner(k, 0) * under)
            nt.append(e1[k] + corner(k, 3) * over + corner(k, 2) * under)
        bs, ts = nb, nt
    for k in range(NG):
        bpad[pl.ds(k * 16, 16), :] = bs[k]
        tpad[pl.ds(k * 16 + 16, 16), :] = ts[k]
    bpad[pl.ds(NG * 16, 16), :] = zero
    tpad[pl.ds(0, 16), :] = zero
    over = bpad[pl.ds(pl.multiple_of(g * 16 + 16, 8), 16), :]
    under = tpad[pl.ds(pl.multiple_of(g * 16, 8), 16), :]

    def update(i, _):
        s = pl.ds(i * 16, 16)
        top = jnp.broadcast_to(binv_v[pl.ds(i * 32 + 31, 1), :], (16, 128))
        bot = jnp.broadcast_to(binv_v[pl.ds(i * 32, 1), :], (16, 128))
        send3[s, :] = send3[s, :] + top * over + bot * under
        return 0

    lax.fori_loop(0, NL, update, 0)
    send_all(2, send3, x3, 16, 16)
    own(send3, x3, 16, 16)

    levels(CUT[1], CUT[2])

    wait_all(2, send3, x3, 16, 16)
    g3 = mats_v[pl.ds(224, 192), :]
    h2 = mats_v[pl.ds(416, 64), :]
    for h in range(4):
        zs = []
        for y in (2 * h, 2 * h + 1):
            s2 = jnp.concatenate([x3[pl.ds(y, NP, stride=16), :], x3[pl.ds(8 + y, NP, stride=16), :]], axis=0)
            hi, lo = split(s2)
            vv = dot_t(jnp.concatenate([hi, lo, hi], axis=0), g3)
            vr, vi = vv[:, :128], vv[:, 128:]
            zs.append(jnp.concatenate([vr * twr + vi * twi, vi * twr - vr * twi], axis=0))
        hi, lo = split(jnp.concatenate(zs, axis=1))
        both = dot(h2, hi)
        pr = both[:32] + both[32:] + dot(h2[:32], lo)
        for n, y in enumerate((2 * h, 2 * h + 1)):
            send4[pl.ds(y, NP, stride=8), :] = pr[:, 128 * n:128 * n + 128]
    send_all(3, send4, pres_v, 8, 8)
    own(send4, pres_v, 8, 8)

    levels(CUT[2], NL // 2)

    @pl.when(not_last)
    def _():
        w_msg(me).wait_send()

    wait_all(3, send4, pres_v, 8, 8)


def write_body(out_v, pres_v, out_h, pres_h, sem):
    copies = [pltpu.make_async_copy(pres_v, pres_h, sem.at[8])]
    for i in range(8):
        s = pl.ds(i * 4 * LVL, 4 * LVL)
        copies.append(pltpu.make_async_copy(out_v.at[s], out_h.at[s], sem.at[i]))
    for c in copies:
        c.start()
    for c in copies:
        c.wait()


CUT = (6, 8, 14)


def body(bins, u, w, fall, kern, redi, ids, counts, binv):
    mats, tw = tables()
    vmem = lambda rows, cols=128, t=F32: pltpu.VMEM((rows, cols), t)
    dma = pltpu.SemaphoreType.DMA
    out, pres = pl.pallas_call(
        kernel_body,
        out_shape=(pltpu.VMEM((NL * LVL, 128), F32), pltpu.VMEM((NL * 8, 128), F32)),
        in_specs=[pl.BlockSpec(memory_space=pltpu.HBM)] * 11,
        out_specs=[pl.BlockSpec(memory_space=pltpu.VMEM)] * 2,
        scratch_shapes=[
            vmem((NL + 1) * LVL), vmem(256), vmem(256), vmem(1024), vmem(480, 256, BF16), vmem(128, 256),
            vmem(NB, NB), vmem(NB, NB), vmem(1, 64, jnp.int32), vmem(1, NB), vmem(1, 1, jnp.int32), vmem(2 * NBP, 3 * NBP), vmem(LVL),
            vmem(512), vmem(512), vmem(512), vmem(512), vmem(512), vmem(512), vmem(256), vmem(256),
            vmem(32), vmem(NG * 32), vmem(8), vmem(NG * 8), vmem((NG + 1) * 16), vmem((NG + 1) * 16),
            vmem(8), vmem(LVL), vmem(LVL), vmem(128), vmem(128), vmem(128), vmem(128), vmem(128), vmem(128), vmem(128),
            vmem(NBP * 8), vmem(LVL), vmem(8),
            dma((10,)), dma((8,)),
            dma((4, NP)), dma((4, NP)), dma((NG,)), dma((NG,)), dma((NG,)), dma((NG,)), dma((6,)), dma((6,)), dma, dma((NP,)),
        ],
        compiler_params=pltpu.CompilerParams(collective_id=0, has_side_effects=True, vmem_limit_bytes=62300000),
        name="slab_step",
    )(
        bins.reshape(NL * LVL, 128), u.reshape(256, 128), w.reshape(256, 128), binv.reshape(1024, 128),
        jnp.asarray(mats), jnp.asarray(tw), kern, redi, ids, fall.reshape(1, NB), counts,
    )
    out, pres = pl.pallas_call(
        write_body,
        out_shape=(jax.ShapeDtypeStruct((NL * LVL, 128), F32), jax.ShapeDtypeStruct((NL * 8, 128), F32)),
        in_specs=[pl.BlockSpec(memory_space=pltpu.VMEM)] * 2,
        out_specs=[pl.BlockSpec(memory_space=pl.ANY)] * 2,
        scratch_shapes=[dma((9,))],
        compiler_params=pltpu.CompilerParams(vmem_limit_bytes=1024 * 1024),
        name="write_out",
    )(out, pres)
    return out.reshape(NL, NB, 8, 128), pres.reshape(NL, 8, 128)


def solution(mesh):
    return jax.shard_map(
        body,
        mesh=mesh,
        in_specs=(
            P("gz", None, None, "gx"),
            P("gz", None, "gx"),
            P("gz", None, "gx"),
            P(),
            P(),
            P(),
            P("gz", "gx"),
            P("gz", "gx"),
            P("gz", None, "gx"),
        ),
        out_specs=(P("gz", None, None, "gx"), P("gz", None, "gx")),
        check_vma=False,
    )
```

```python
import functools
import math

import jax
import jax.numpy as jnp
import numpy as np
from jax import lax
from jax.experimental import pallas as pl
from jax.experimental.pallas import tpu as pltpu
from jax.sharding import PartitionSpec as P

F32 = jnp.float32
BF16 = jnp.bfloat16
MESH = pl.DeviceIdType.MESH
NB = 33
NBP = 48
NL = 32
NG = 8
NP = 32
LVL = NB * 8


def halves(x):
    hi = np.asarray(np.asarray(x, np.float32), jnp.bfloat16)
    lo = np.asarray(np.asarray(x - hi.astype(np.float64), np.float32), jnp.bfloat16)
    return hi, lo


def tables():
    p = np.arange(32)
    c = np.arange(128)
    pj = 2.0 * math.pi / 32 * (p[:, None] * c[None, :] % 32)
    cj = 2.0 * math.pi / 4096 * (c[:, None] * c[None, :])
    cos, sin = np.cos(pj), np.sin(pj)
    e_hi, e_lo = halves(np.concatenate([cos, -sin], 1))
    e3 = np.concatenate([e_hi, e_hi, e_lo], 0)
    fwd = np.concatenate([np.concatenate([cos, sin], 1), np.concatenate([-sin, cos], 1)], 0)
    f2 = np.concatenate(halves(fwd), 0)
    g = np.concatenate([np.concatenate([cos, sin], 1), np.concatenate([-sin, cos], 1)], 0)
    g_hi, g_lo = halves(g)
    g3 = np.concatenate([g_hi, g_hi, g_lo], 0)
    h2 = np.concatenate(halves(np.concatenate([cos, -sin], 1) / 4096.0), 0)
    mats = np.concatenate([e3, f2, g3, h2], 0)
    tw = np.concatenate([np.cos(cj), -np.sin(cj)], 1).astype(np.float32)
    return mats, tw


def split(x):
    hi = x.astype(BF16)
    lo = (x - hi.astype(F32)).astype(BF16)
    return hi, lo


def dot(a, b):
    return jnp.dot(a, b, preferred_element_type=F32)


def dot_t(a, b):
    return lax.dot_general(a, b, (((0,), (0,)), ((), ())), preferred_element_type=F32)


def kernel_body(
    bins_h, u_h, w_h, binv_h, mats_h, tw_h, kern_h, redi_h, ids_h, fall_h, cnt_h,
    out_v, pres_v,
    bins_v, u_v, w_v, binv_v, mats_v, tw_v, kern_v, redi_v, ids_v, fall_v, cnt_v, coll_v, fall_t,
    send1, x1, send2, x2, send3, x3, send4, wtop,
    esend, edges, csend, corners,
    wlow, zlo, zhi, send_f, send_l, halo_r, halo_l, prior,
    adv, fz, mask_v,
    in_sem, bin_sem,
    a2a_send, a2a_recv, e_send, e_recv, c_send, c_recv, h_send, h_recv, w_send, w_recv,
):
    me = lax.axis_index("gx")
    g = lax.axis_index("gz")
    right = {"gx": lax.rem(me + 1, NP)}
    left = {"gx": lax.rem(me + NP - 1, NP)}
    above = {"gz": lax.rem(g + 1, NG)}
    below = {"gz": lax.rem(g + NG - 1, NG)}

    lane = lax.broadcasted_iota(jnp.int32, (8, 128), 1)
    sub = lax.broadcasted_iota(jnp.int32, (8, 128), 0)

    barrier = pltpu.get_barrier_semaphore()

    def peer_of(t):
        half = (t + 1) // 2
        odd = lax.rem(t, 2)
        o = 16 + odd * half - (1 - odd) * half
        return lax.rem(me + o, NP)

    def greet(gx, gz):
        pl.semaphore_signal(barrier, inc=1, device_id={"gx": gx, "gz": gz}, device_id_type=MESH)

    def greet_low(o, _):
        greet(o, lax.rem(g + NG - 1, NG))
        return 0

    not_first = g > 0
    not_last = g < NG - 1
    takes_w = (me == 0) & not_first
    near = [(d, (g + d >= 0) & (g + d < NG)) for d in (3, -3, 2, -2, 1, -1)]

    loads = [
        pltpu.make_async_copy(s, d, in_sem.at[i])
        for i, (s, d) in enumerate(
            [(u_h, u_v), (w_h, w_v), (binv_h, binv_v), (mats_h, mats_v), (tw_h, tw_v),
             (kern_h, kern_v), (redi_h, redi_v), (ids_h, ids_v), (fall_h, fall_v), (cnt_h, cnt_v)]
        )
    ]
    loads[0].start()
    loads[1].start()
    for t in range(NP - 1):
        half = (t + 1) // 2
        greet(lax.rem(me + (16 + half if t % 2 else 16 - half), NP), g)
    for d, there in near:
        @pl.when(there)
        def _(d=d):
            greet(me, g + d)

    @pl.when(takes_w)
    def _():
        lax.fori_loop(1, NP, greet_low, 0)

    bin_loads = [
        pltpu.make_async_copy(bins_h.at[pl.ds(i * 4 * LVL, 4 * LVL)], bins_v.at[pl.ds(i * 4 * LVL, 4 * LVL)], bin_sem.at[i])
        for i in range(8)
    ]
    for i in range(8):
        bin_loads[i].start()
    for c in loads[2:]:
        c.start()
    loads[0].wait()
    loads[1].wait()

    def tile_div(q, w_under):
        u = u_v[pl.ds(q * 8, 8), :]
        before = jnp.where(lane == 0, 0.0, pltpu.roll(u, 1, 1))
        d = (u - before) + (w_v[pl.ds(q * 8, 8), :] - w_under)
        row = jnp.sum(jnp.where(lane == sub, jnp.broadcast_to(u[:, 127:128], (8, 128)), 0.0), axis=0, keepdims=True)
        send1[pl.ds(q * 16, 8), :] = d
        send1[pl.ds(q * 16 + 8, 8), :] = jnp.broadcast_to(row, (8, 128))

    tile_div(0, jnp.zeros((8, 128), F32))
    for q in range(1, NL):
        tile_div(q, w_v[pl.ds(q * 8 - 8, 8), :])

    @pl.when(jnp.logical_not(takes_w))
    def _():
        wtop[...] = jnp.zeros((256, 128), F32)

    extra = jnp.where(not_last & (me != 0), 1, 0)
    n_near = jnp.minimum(g, 3) + jnp.minimum(NG - 1 - g, 3)
    pl.semaphore_wait(barrier, NP - 1 + n_near + extra)

    def w_msg(p):
        return pltpu.make_async_remote_copy(
            src_ref=w_v.at[pl.ds(248, 8)], dst_ref=wtop.at[pl.ds(pl.multiple_of(p * 8, 8), 8)],
            send_sem=w_send, recv_sem=w_recv.at[p], device_id={"gx": me * 0, "gz": lax.rem(g + 1, NG)}, device_id_type=MESH)

    @pl.when(not_last)
    def _():
        w_msg(me).start()

    def msg(stage, src, dst, rows, peer, at):
        s0 = pl.multiple_of(peer * at, 8)
        d0 = pl.multiple_of(me * at, 8)
        return pltpu.make_async_remote_copy(
            src_ref=src.at[pl.ds(s0, rows)], dst_ref=dst.at[pl.ds(d0, rows)],
            send_sem=a2a_send.at[stage, peer], recv_sem=a2a_recv.at[stage, me],
            device_id={"gx": peer}, device_id_type=MESH)

    def send_all(stage, src, dst, rows, at):
        def step(t, _):
            msg(stage, src, dst, rows, peer_of(t), at).start()
            return 0
        lax.fori_loop(0, NP - 1, step, 0)

    def wait_all(stage, src, dst, rows, at):
        def step(t, _):
            peer = lax.rem(me + t + 1, NP)
            d0 = pl.multiple_of(peer * at, 8)
            pltpu.make_async_remote_copy(
                src_ref=src.at[pl.ds(d0, rows)], dst_ref=dst.at[pl.ds(d0, rows)],
                send_sem=a2a_send.at[stage, peer], recv_sem=a2a_recv.at[stage, peer],
                device_id={"gx": peer}, device_id_type=MESH).wait()
            return 0
        lax.fori_loop(0, NP - 1, step, 0)

    def own(src, dst, rows, at):
        m0 = pl.multiple_of(me * at, 8)
        dst[pl.ds(m0, rows), :] = src[pl.ds(m0, rows), :]

    send_all(0, send1, x1, 9, 16)
    own(send1, x1, 16, 16)

    bin_loads[7].wait()
    bin_loads[0].wait()
    z_up = pltpu.make_async_remote_copy(
        src_ref=bins_v.at[pl.ds(31 * LVL, LVL)], dst_ref=zlo, send_sem=h_send.at[1], recv_sem=h_recv.at[1],
        device_id=above, device_id_type=MESH)
    z_down = pltpu.make_async_remote_copy(
        src_ref=bins_v.at[pl.ds(0, LVL)], dst_ref=zhi, send_sem=h_send.at[2], recv_sem=h_recv.at[2],
        device_id=below, device_id_type=MESH)
    w_up = pltpu.make_async_remote_copy(
        src_ref=w_v.at[pl.ds(248, 8)], dst_ref=wlow, send_sem=h_send.at[0], recv_sem=h_recv.at[0],
        device_id=above, device_id_type=MESH)

    @pl.when(not_last)
    def _():
        w_up.start()
        z_up.start()

    @pl.when(not_first)
    def _():
        z_down.start()

    @pl.when(jnp.logical_not(not_first))
    def _():
        wlow[...] = jnp.zeros((8, 128), F32)
        zlo[...] = jnp.zeros((LVL, 128), F32)

    @pl.when(jnp.logical_not(not_last))
    def _():
        zhi[...] = jnp.zeros((LVL, 128), F32)

    loads[2].wait()
    csend[...] = jnp.zeros((8, 128), F32)
    for i, r in enumerate((0, 31, 31 * 32, 31 * 32 + 31)):
        csend[pl.ds(i, 1), :] = binv_v[pl.ds(r, 1), :]

    def corner_msg(d, group):
        return pltpu.make_async_remote_copy(
            src_ref=csend, dst_ref=corners.at[pl.ds(pl.multiple_of((group + 3) * 8, 8), 8)],
            send_sem=c_send.at[d + 3], recv_sem=c_recv.at[group], device_id={"gz": lax.rem(g + d + NG, NG)}, device_id_type=MESH)

    def edge_msg(d, group, toward):
        first = 16 if abs(d) > 1 and toward > 0 else 0
        rows = 32 if abs(d) == 1 else 16
        return pltpu.make_async_remote_copy(
            src_ref=esend.at[pl.ds(first, rows)], dst_ref=edges.at[pl.ds(pl.multiple_of((group + 3) * 32 + first, 8), rows)],
            send_sem=e_send.at[d + 3], recv_sem=e_recv.at[group], device_id={"gz": lax.rem(g + d + NG, NG)}, device_id_type=MESH)

    for lo in (0, NG + 3):
        edges[pl.ds(lo * 32, 96), :] = jnp.zeros((96, 128), F32)
        corners[pl.ds(lo * 8, 24), :] = jnp.zeros((24, 128), F32)
    corners[pl.ds(pl.multiple_of((g + 3) * 8, 8), 8), :] = csend[...]
    for d, there in near:
        @pl.when(there)
        def _(d=d):
            corner_msg(d, g).start()

    for i in range(1, 7):
        bin_loads[i].wait()

    turned = lax.rem(lane + 1, 128)

    def columns(vs):
        items = [(v, 1) for v in vs]
        while len(items) > 1:
            merged = []
            for n in range(0, len(items) - 1, 2):
                (a, ca), (b, cb) = items[n], items[n + 1]
                merged.append((jnp.where(turned < 2 * ca, a, pltpu.roll(b, 2 * ca, 1)), ca + cb))
            if len(items) % 2:
                merged.append(items[-1])
            items = merged
        return items[0][0]

    even = lax.rem(lane, 2) == 0

    def pack(i, _):
        sides = []
        for r in range(2):
            tiles = [bins_v[pl.ds((2 * i + r) * LVL + m * 8, 8), :] for m in range(NB)]
            sides.append(columns(tiles + [u_v[pl.ds((2 * i + r) * 8, 8), :]]))
        other = pltpu.roll(sides[1], 1, 1)
        send_f[pl.ds(i * 8, 8), :] = jnp.where(even, sides[0], other)
        send_l[pl.ds(i * 8, 8), :] = jnp.where(even, other, sides[0])
        return 0

    lax.fori_loop(0, NL // 2, pack, 0)
    x_copies = [
        pltpu.make_async_remote_copy(src_ref=s, dst_ref=d, send_sem=h_send.at[i], recv_sem=h_recv.at[i], device_id=to, device_id_type=MESH)
        for i, s, d, to in ((3, send_f, halo_r, left), (4, send_l, halo_l, right))
    ]
    for c in x_copies:
        c.start()

    for c in loads[3:]:
        c.wait()

    block = lax.broadcasted_iota(jnp.int32, (64, 64), 0)
    slot = lax.broadcasted_iota(jnp.int32, (64, 64), 1)
    hits = (jnp.broadcast_to(ids_v[...], (64, 64)) == block) & (slot < jnp.broadcast_to(cnt_v[...], (64, 64)))
    marks = jnp.max(jnp.where(hits, 1.0, 0.0), axis=1, keepdims=True)
    col_block = lax.broadcasted_iota(jnp.int32, (16, 128), 1) // 8
    row_block = lax.broadcasted_iota(jnp.int32, (16, 128), 0)
    for bz in range(4):
        wide = jnp.broadcast_to(marks[bz * 16:bz * 16 + 16, :], (16, 128))
        mask_v[pl.ds(bz, 1), :] = jnp.sum(jnp.where(col_block == row_block, wide, 0.0), axis=0, keepdims=True)

    adv[...] = jnp.zeros((NBP * 8, 128), F32)
    coll_v[...] = jnp.zeros((2 * NBP, 3 * NBP), F32)
    pos = lax.broadcasted_iota(jnp.int32, (NB, 3 * NBP), 1)
    row = lax.broadcasted_iota(jnp.int32, (NB, 3 * NBP), 0)
    pick_hi = jnp.where((pos == row) | (pos == row + 2 * NBP), 1.0, 0.0).astype(BF16)
    pick_lo = jnp.where(pos == row + NBP, 1.0, 0.0).astype(BF16)
    for n, ref in enumerate((kern_v, redi_v)):
        hi, lo = split(ref[...])
        coll_v[pl.ds(n * NBP, NB), :] = dot_t(hi, pick_hi) + dot_t(lo, pick_lo)
    for m in range(NB):
        fall_t[pl.ds(m * 8, 8), :] = jnp.broadcast_to(fall_v[:, m:m + 1], (8, 128))

    def level(z, i, r):
        u = u_v[pl.ds(z * 8, 8), :]
        u_pos, u_neg = jnp.maximum(u, 0.0), jnp.minimum(u, 0.0)
        w = w_v[pl.ds(z * 8, 8), :]
        hr = halo_r[pl.ds(i * 8, 8), :]
        pf = prior[pl.ds(i * 8, 8), :]
        base = z * LVL
        for m in range(NB):
            k = 2 * m + r
            kl = (k + 127) % 128
            b = bins_v[pl.ds(base + m * 8, 8), :]
            up = bins_v[pl.ds(base + LVL + m * 8, 8), :]
            nxt = jnp.where(lane == 127, jnp.broadcast_to(hr[:, k:k + 1], (8, 128)), pltpu.roll(b, 127, 1))
            flux = u_pos * b + u_neg * nxt
            prev = jnp.where(lane == 0, jnp.broadcast_to(pf[:, kl:kl + 1], (8, 128)), pltpu.roll(flux, 1, 1))
            c = w - fall_t[pl.ds(m * 8, 8), :]
            top = jnp.maximum(c, 0.0) * b + jnp.minimum(c, 0.0) * up
            s = pl.ds(m * 8, 8)
            adv[s, :] = b - (flux - prev) - (top - fz[s, :])
            fz[s, :] = top
        mark = jnp.broadcast_to(mask_v[pl.ds(z // 8, 1), :], (NBP, 128))
        grow_w = coll_v[pl.ds(0, NBP), :].astype(BF16)
        redi_w = coll_v[pl.ds(NBP, NBP), :].astype(BF16)
        for h in range(4):
            ys = (2 * h, 2 * h + 1)
            v = jnp.concatenate([adv[pl.ds(y, NBP, stride=8), :] for y in ys], axis=1)
            hi, lo = split(v)
            rate = dot(grow_w, jnp.concatenate([hi, hi, lo], axis=0))
            hi, lo = split(v * rate)
            tend = dot(redi_w, jnp.concatenate([hi, hi, lo], axis=0))
            for n, y in enumerate(ys):
                part = slice(128 * n, 128 * n + 128)
                new = v[:, part] + tend[:, part] * mark
                out_v[pl.ds(base + y, NB, stride=8), :] = new[:NB]

    def levels(first, last):
        def step(i, _):
            level(2 * i, i, 0)
            level(2 * i + 1, i, 1)
            return 0
        lax.fori_loop(first, last, step, 0)

    wait_all(0, send1, x1, 9, 16)

    @pl.when(takes_w)
    def _():
        def step(p, _):
            w_msg(p).wait_recv()
            return 0
        lax.fori_loop(0, NP, step, 0)

    borders = x1[pl.ds(8, NP, stride=16), :]
    borders = pltpu.roll(borders, 1, 0)
    lane32 = lax.broadcasted_iota(jnp.int32, (32, 128), 1)
    e3 = mats_v[pl.ds(0, 96), :]
    f2 = mats_v[pl.ds(96, 128), :]
    twr = tw_v[:, 0:128]
    twi = tw_v[:, 128:256]
    for h in range(4):
        us = []
        for y in (2 * h, 2 * h + 1):
            xy = x1[pl.ds(y, NP, stride=16), :] - wtop[pl.ds(y, NP, stride=8), :]
            shifted = borders if y == 0 else pltpu.roll(borders, 128 - y, 1)
            xy = xy - jnp.where(lane32 == 0, shifted, 0.0)
            hi, lo = split(xy)
            yy = dot_t(jnp.concatenate([hi, lo, hi], axis=0), e3)
            yr, yi = yy[:, :128], yy[:, 128:]
            us.append(jnp.concatenate([yr * twr - yi * twi, yr * twi + yi * twr], axis=0))
        hi, lo = split(jnp.concatenate(us, axis=1))
        both = dot(f2, hi)
        spec = both[:64] + both[64:] + dot(f2[:64], lo)
        for n, y in enumerate((2 * h, 2 * h + 1)):
            part = slice(128 * n, 128 * n + 128)
            send2[pl.ds(y, NP, stride=16), :] = spec[:32, part]
            send2[pl.ds(8 + y, NP, stride=16), :] = spec[32:, part]
    send_all(1, send2, x2, 16, 16)
    own(send2, x2, 16, 16)

    @pl.when(not_last)
    def _():
        z_up.wait_send()
        w_up.wait_send()
        z_down.wait_recv()

    @pl.when(not_first)
    def _():
        z_up.wait_recv()
        w_up.wait_recv()
        z_down.wait_send()

    for c in x_copies:
        c.wait()

    def prior_step(i, _):
        s = pl.ds(i * 8, 8)
        edge = halo_l[s, :]
        speed = jnp.where(even, jnp.broadcast_to(edge[:, 66:67], (8, 128)), jnp.broadcast_to(edge[:, 65:66], (8, 128)))
        prior[s, :] = jnp.maximum(speed, 0.0) * edge + jnp.minimum(speed, 0.0) * pltpu.roll(send_f[s, :], 127, 1)
        return 0

    lax.fori_loop(0, NL // 2, prior_step, 0)

    w_low = jnp.where(not_first, wlow[...], 0.0)

    def low_face(m, _):
        s = pl.ds(m * 8, 8)
        c = w_low - fall_t[s, :]
        fz[s, :] = jnp.maximum(c, 0.0) * jnp.where(not_first, zlo[s, :], 0.0) + jnp.minimum(c, 0.0) * bins_v[s, :]
        bins_v[pl.ds(NL * LVL + m * 8, 8), :] = jnp.where(not_last, zhi[s, :], 0.0)
        return 0

    lax.fori_loop(0, NB, low_face, 0)


    levels(0, CUT[0])

    wait_all(1, send2, x2, 16, 16)

    def apply_rows(rows):
        accs = [None] * len(rows)
        for j in range(NL):
            s = x2[pl.ds(j * 16, 16), :]
            for n, i in enumerate(rows):
                b = jnp.broadcast_to(binv_v[pl.ds(i * 32 + j, 1), :], (16, 128))
                accs[n] = b * s if accs[n] is None else accs[n] + b * s
        return accs

    low, high = apply_rows((0, 31))
    esend[pl.ds(0, 16), :] = low
    esend[pl.ds(16, 16), :] = high
    edges[pl.ds(pl.multiple_of((g + 3) * 32, 8), 32), :] = esend[...]
    for d, there in near:
        @pl.when(there)
        def _(d=d):
            edge_msg(d, g, d).start()

    def solve_step(t, _):
        rows = [t * 4 + n for n in range(4)]
        for i, acc in zip(rows, apply_rows(rows)):
            send3[pl.ds(i * 16, 16), :] = acc
        return 0

    lax.fori_loop(0, NL // 4, solve_step, 0)
    levels(CUT[0], CUT[1])
    for d, there in near:
        @pl.when(there)
        def _(d=d):
            corner_msg(d, g).wait_send()
            corner_msg(d, g + d).wait_recv()
            edge_msg(d, g, d).wait_send()
            edge_msg(d, g + d, -d).wait_recv()

    def e0(d):
        return edges[pl.ds(pl.multiple_of((g + 3 + d) * 32, 8), 16), :]

    def e1(d):
        return edges[pl.ds(pl.multiple_of((g + 3 + d) * 32 + 16, 8), 16), :]

    def corner(d, i):
        return jnp.broadcast_to(corners[pl.ds((g + 3 + d) * 8 + i, 1), :], (16, 128))

    def low_edge(d, over, under):
        return e0(d) + corner(d, 1) * over + corner(d, 0) * under

    def high_edge(d, over, under):
        return e1(d) + corner(d, 3) * over + corner(d, 2) * under

    over = low_edge(1, low_edge(2, e0(3), e1(1)), high_edge(0, e0(1), e1(-1)))
    under = high_edge(-1, low_edge(0, e0(1), e1(-1)), high_edge(-2, e0(-1), e1(-3)))

    def update(i, _):
        s = pl.ds(i * 16, 16)
        top = jnp.broadcast_to(binv_v[pl.ds(i * 32 + 31, 1), :], (16, 128))
        bot = jnp.broadcast_to(binv_v[pl.ds(i * 32, 1), :], (16, 128))
        send3[s, :] = send3[s, :] + top * over + bot * under
        return 0

    lax.fori_loop(0, NL, update, 0)
    send_all(2, send3, x3, 16, 16)
    own(send3, x3, 16, 16)

    levels(CUT[1], CUT[2])

    wait_all(2, send3, x3, 16, 16)
    g3 = mats_v[pl.ds(224, 192), :]
    h2 = mats_v[pl.ds(416, 64), :]
    for h in range(4):
        zs = []
        for y in (2 * h, 2 * h + 1):
            s2 = jnp.concatenate([x3[pl.ds(y, NP, stride=16), :], x3[pl.ds(8 + y, NP, stride=16), :]], axis=0)
            hi, lo = split(s2)
            vv = dot_t(jnp.concatenate([hi, lo, hi], axis=0), g3)
            vr, vi = vv[:, :128], vv[:, 128:]
            zs.append(jnp.concatenate([vr * twr + vi * twi, vi * twr - vr * twi], axis=0))
        hi, lo = split(jnp.concatenate(zs, axis=1))
        both = dot(h2, hi)
        pr = both[:32] + both[32:] + dot(h2[:32], lo)
        for n, y in enumerate((2 * h, 2 * h + 1)):
            send4[pl.ds(y, NP, stride=8), :] = pr[:, 128 * n:128 * n + 128]
    send_all(3, send4, pres_v, 8, 8)
    own(send4, pres_v, 8, 8)

    levels(CUT[2], NL // 2)

    @pl.when(not_last)
    def _():
        w_msg(me).wait_send()

    wait_all(3, send4, pres_v, 8, 8)


def write_body(out_v, pres_v, out_h, pres_h, sem):
    copies = [pltpu.make_async_copy(pres_v, pres_h, sem.at[8])]
    for i in range(8):
        s = pl.ds(i * 4 * LVL, 4 * LVL)
        copies.append(pltpu.make_async_copy(out_v.at[s], out_h.at[s], sem.at[i]))
    for c in copies:
        c.start()
    for c in copies:
        c.wait()


CUT = (5, 8, 14)


def body(bins, u, w, fall, kern, redi, ids, counts, binv):
    mats, tw = tables()
    vmem = lambda rows, cols=128, t=F32: pltpu.VMEM((rows, cols), t)
    dma = pltpu.SemaphoreType.DMA
    out, pres = pl.pallas_call(
        kernel_body,
        out_shape=(pltpu.VMEM((NL * LVL, 128), F32), pltpu.VMEM((NL * 8, 128), F32)),
        in_specs=[pl.BlockSpec(memory_space=pltpu.HBM)] * 11,
        out_specs=[pl.BlockSpec(memory_space=pltpu.VMEM)] * 2,
        scratch_shapes=[
            vmem((NL + 1) * LVL), vmem(256), vmem(256), vmem(1024), vmem(480, 256, BF16), vmem(128, 256),
            vmem(NB, NB), vmem(NB, NB), vmem(1, 64, jnp.int32), vmem(1, NB), vmem(1, 1, jnp.int32), vmem(2 * NBP, 3 * NBP), vmem(LVL),
            vmem(512), vmem(512), vmem(512), vmem(512), vmem(512), vmem(512), vmem(256), vmem(256),
            vmem(32), vmem((NG + 6) * 32), vmem(8), vmem((NG + 6) * 8),
            vmem(8), vmem(LVL), vmem(LVL), vmem(128), vmem(128), vmem(128), vmem(128), vmem(128),
            vmem(NBP * 8), vmem(LVL), vmem(8),
            dma((10,)), dma((8,)),
            dma((4, NP)), dma((4, NP)), dma((NG,)), dma((NG,)), dma((NG,)), dma((NG,)), dma((6,)), dma((6,)), dma, dma((NP,)),
        ],
        compiler_params=pltpu.CompilerParams(collective_id=0, has_side_effects=True, vmem_limit_bytes=62300000),
        name="slab_step",
    )(
        bins.reshape(NL * LVL, 128), u.reshape(256, 128), w.reshape(256, 128), binv.reshape(1024, 128),
        jnp.asarray(mats), jnp.asarray(tw), kern, redi, ids, fall.reshape(1, NB), counts,
    )
    out, pres = pl.pallas_call(
        write_body,
        out_shape=(jax.ShapeDtypeStruct((NL * LVL, 128), F32), jax.ShapeDtypeStruct((NL * 8, 128), F32)),
        in_specs=[pl.BlockSpec(memory_space=pltpu.VMEM)] * 2,
        out_specs=[pl.BlockSpec(memory_space=pl.ANY)] * 2,
        scratch_shapes=[dma((9,))],
        compiler_params=pltpu.CompilerParams(vmem_limit_bytes=1024 * 1024),
        name="write_out",
    )(out, pres)
    return out.reshape(NL, NB, 8, 128), pres.reshape(NL, 8, 128)


def solution(mesh):
    return jax.shard_map(
        body,
        mesh=mesh,
        in_specs=(
            P("gz", None, None, "gx"),
            P("gz", None, "gx"),
            P("gz", None, "gx"),
            P(),
            P(),
            P(),
            P("gz", "gx"),
            P("gz", "gx"),
            P("gz", None, "gx"),
        ),
        out_specs=(P("gz", None, None, "gx"), P("gz", None, "gx")),
        check_vma=False,
    )
```

```python
import functools
import math

import jax
import jax.numpy as jnp
import numpy as np
from jax import lax
from jax.experimental import pallas as pl
from jax.experimental.pallas import tpu as pltpu
from jax.sharding import PartitionSpec as P

F32 = jnp.float32
BF16 = jnp.bfloat16
MESH = pl.DeviceIdType.MESH
NB = 33
NBP = 48
NL = 32
NG = 8
NP = 32
LVL = NB * 8


def halves(x):
    hi = np.asarray(np.asarray(x, np.float32), jnp.bfloat16)
    lo = np.asarray(np.asarray(x - hi.astype(np.float64), np.float32), jnp.bfloat16)
    return hi, lo


def tables():
    p = np.arange(32)
    c = np.arange(128)
    pj = 2.0 * math.pi / 32 * (p[:, None] * c[None, :] % 32)
    cj = 2.0 * math.pi / 4096 * (c[:, None] * c[None, :])
    cos, sin = np.cos(pj), np.sin(pj)
    e_hi, e_lo = halves(np.concatenate([cos, -sin], 1))
    e3 = np.concatenate([e_hi, e_hi, e_lo], 0)
    fwd = np.concatenate([np.concatenate([cos, sin], 1), np.concatenate([-sin, cos], 1)], 0)
    f2 = np.concatenate(halves(fwd), 0)
    g = np.concatenate([np.concatenate([cos, sin], 1), np.concatenate([-sin, cos], 1)], 0)
    g_hi, g_lo = halves(g)
    g3 = np.concatenate([g_hi, g_hi, g_lo], 0)
    h2 = np.concatenate(halves(np.concatenate([cos, -sin], 1) / 4096.0), 0)
    mats = np.concatenate([e3, f2, g3, h2], 0)
    tw = np.concatenate([np.cos(cj), -np.sin(cj)], 1).astype(np.float32)
    return mats, tw


def split(x):
    hi = x.astype(BF16)
    lo = (x - hi.astype(F32)).astype(BF16)
    return hi, lo


def dot(a, b):
    return jnp.dot(a, b, preferred_element_type=F32)


def dot_t(a, b):
    return lax.dot_general(a, b, (((0,), (0,)), ((), ())), preferred_element_type=F32)


def kernel_body(
    bins_h, u_h, w_h, binv_h, mats_h, tw_h, kern_h, redi_h, ids_h, fall_h, cnt_h,
    out_v, pres_v,
    bins_v, u_v, w_v, binv_v, mats_v, tw_v, kern_v, redi_v, ids_v, fall_v, cnt_v, coll_v, fall_t,
    send1, x1, send2, x2, send3, x3, send4, wtop,
    esend, edges, csend, corners,
    wlow, zlo, zhi, send_f, send_l, halo_r, halo_l, prior,
    adv, fz, mask_v,
    in_sem, bin_sem,
    a2a_send, a2a_recv, e_send, e_recv, c_send, c_recv, h_send, h_recv, w_send, w_recv,
):
    me = lax.axis_index("gx")
    g = lax.axis_index("gz")
    right = {"gx": lax.rem(me + 1, NP)}
    left = {"gx": lax.rem(me + NP - 1, NP)}
    above = {"gz": lax.rem(g + 1, NG)}
    below = {"gz": lax.rem(g + NG - 1, NG)}

    lane = lax.broadcasted_iota(jnp.int32, (8, 128), 1)
    sub = lax.broadcasted_iota(jnp.int32, (8, 128), 0)

    barrier = pltpu.get_barrier_semaphore()

    def peer_of(t):
        half = (t + 1) // 2
        odd = lax.rem(t, 2)
        o = 16 + odd * half - (1 - odd) * half
        return lax.rem(me + o, NP)

    def greet(gx, gz):
        pl.semaphore_signal(barrier, inc=1, device_id={"gx": gx, "gz": gz}, device_id_type=MESH)

    def greet_low(o, _):
        greet(o, lax.rem(g + NG - 1, NG))
        return 0

    not_first = g > 0
    not_last = g < NG - 1
    takes_w = (me == 0) & not_first
    near = [(d, (g + d >= 0) & (g + d < NG)) for d in (3, -3, 2, -2, 1, -1)]

    loads = [
        pltpu.make_async_copy(s, d, in_sem.at[i])
        for i, (s, d) in enumerate(
            [(u_h, u_v), (w_h, w_v), (binv_h, binv_v), (mats_h, mats_v), (tw_h, tw_v),
             (kern_h, kern_v), (redi_h, redi_v), (ids_h, ids_v), (fall_h, fall_v), (cnt_h, cnt_v)]
        )
    ]
    loads[0].start()
    loads[1].start()
    for t in range(NP - 1):
        half = (t + 1) // 2
        greet(lax.rem(me + (16 + half if t % 2 else 16 - half), NP), g)
    for d, there in near:
        @pl.when(there)
        def _(d=d):
            greet(me, g + d)

    @pl.when(takes_w)
    def _():
        lax.fori_loop(1, NP, greet_low, 0)

    bin_loads = [
        pltpu.make_async_copy(bins_h.at[pl.ds(i * 4 * LVL, 4 * LVL)], bins_v.at[pl.ds(i * 4 * LVL, 4 * LVL)], bin_sem)
        for i in range(8)
    ]
    for i in range(8):
        bin_loads[i].start()
    for c in loads[2:]:
        c.start()
    loads[0].wait()
    loads[1].wait()

    def tile_div(q, w_under):
        u = u_v[pl.ds(q * 8, 8), :]
        before = jnp.where(lane == 0, 0.0, pltpu.roll(u, 1, 1))
        d = (u - before) + (w_v[pl.ds(q * 8, 8), :] - w_under)
        row = jnp.sum(jnp.where(lane == sub, jnp.broadcast_to(u[:, 127:128], (8, 128)), 0.0), axis=0, keepdims=True)
        send1[pl.ds(q * 16, 8), :] = d
        send1[pl.ds(q * 16 + 8, 8), :] = jnp.broadcast_to(row, (8, 128))

    tile_div(0, jnp.zeros((8, 128), F32))
    for q in range(1, NL):
        tile_div(q, w_v[pl.ds(q * 8 - 8, 8), :])

    @pl.when(jnp.logical_not(takes_w))
    def _():
        wtop[...] = jnp.zeros((256, 128), F32)

    extra = jnp.where(not_last & (me != 0), 1, 0)
    n_near = jnp.minimum(g, 3) + jnp.minimum(NG - 1 - g, 3)
    pl.semaphore_wait(barrier, NP - 1 + n_near + extra)

    def w_msg(p):
        return pltpu.make_async_remote_copy(
            src_ref=w_v.at[pl.ds(248, 8)], dst_ref=wtop.at[pl.ds(pl.multiple_of(p * 8, 8), 8)],
            send_sem=w_send, recv_sem=w_recv, device_id={"gx": me * 0, "gz": lax.rem(g + 1, NG)}, device_id_type=MESH)

    @pl.when(not_last)
    def _():
        w_msg(me).start()

    def msg(stage, src, dst, rows, peer, at):
        s0 = pl.multiple_of(peer * at, 8)
        d0 = pl.multiple_of(me * at, 8)
        return pltpu.make_async_remote_copy(
            src_ref=src.at[pl.ds(s0, rows)], dst_ref=dst.at[pl.ds(d0, rows)],
            send_sem=a2a_send.at[stage], recv_sem=a2a_recv.at[stage],
            device_id={"gx": peer}, device_id_type=MESH)

    def send_all(stage, src, dst, rows, at):
        def step(t, _):
            msg(stage, src, dst, rows, peer_of(t), at).start()
            return 0
        lax.fori_loop(0, NP - 1, step, 0)

    def wait_all(stage, src, dst, rows):
        total = pl.ds(0, (NP - 1) * rows)
        pltpu.make_async_remote_copy(
            src_ref=src.at[total], dst_ref=dst.at[total], send_sem=a2a_send.at[stage], recv_sem=a2a_recv.at[stage],
            device_id={"gx": lax.rem(me + 1, NP)}, device_id_type=MESH).wait()

    def own(src, dst, rows, at):
        m0 = pl.multiple_of(me * at, 8)
        dst[pl.ds(m0, rows), :] = src[pl.ds(m0, rows), :]

    send_all(0, send1, x1, 9, 16)
    own(send1, x1, 16, 16)

    pltpu.make_async_copy(bins_h, bins_v.at[pl.ds(0, NL * LVL)], bin_sem).wait()
    z_up = pltpu.make_async_remote_copy(
        src_ref=bins_v.at[pl.ds(31 * LVL, LVL)], dst_ref=zlo, send_sem=h_send.at[1], recv_sem=h_recv.at[1],
        device_id=above, device_id_type=MESH)
    z_down = pltpu.make_async_remote_copy(
        src_ref=bins_v.at[pl.ds(0, LVL)], dst_ref=zhi, send_sem=h_send.at[2], recv_sem=h_recv.at[2],
        device_id=below, device_id_type=MESH)
    w_up = pltpu.make_async_remote_copy(
        src_ref=w_v.at[pl.ds(248, 8)], dst_ref=wlow, send_sem=h_send.at[0], recv_sem=h_recv.at[0],
        device_id=above, device_id_type=MESH)

    @pl.when(not_last)
    def _():
        w_up.start()
        z_up.start()

    @pl.when(not_first)
    def _():
        z_down.start()

    @pl.when(jnp.logical_not(not_first))
    def _():
        wlow[...] = jnp.zeros((8, 128), F32)
        zlo[...] = jnp.zeros((LVL, 128), F32)

    @pl.when(jnp.logical_not(not_last))
    def _():
        zhi[...] = jnp.zeros((LVL, 128), F32)

    loads[2].wait()
    csend[...] = jnp.zeros((8, 128), F32)
    for i, r in enumerate((0, 31, 31 * 32, 31 * 32 + 31)):
        csend[pl.ds(i, 1), :] = binv_v[pl.ds(r, 1), :]

    def corner_msg(d, group, toward):
        return pltpu.make_async_remote_copy(
            src_ref=csend, dst_ref=corners.at[pl.ds(pl.multiple_of((group + 3) * 8, 8), 8)],
            send_sem=c_send.at[d + 3], recv_sem=c_recv.at[toward + 3], device_id={"gz": lax.rem(g + d + NG, NG)}, device_id_type=MESH)

    def edge_msg(d, group, toward):
        first = 16 if abs(d) > 1 and toward > 0 else 0
        rows = 32 if abs(d) == 1 else 16
        return pltpu.make_async_remote_copy(
            src_ref=esend.at[pl.ds(first, rows)], dst_ref=edges.at[pl.ds(pl.multiple_of((group + 3) * 32 + first, 8), rows)],
            send_sem=e_send.at[d + 3], recv_sem=e_recv.at[toward + 3], device_id={"gz": lax.rem(g + d + NG, NG)}, device_id_type=MESH)

    for lo in (0, NG + 3):
        edges[pl.ds(lo * 32, 96), :] = jnp.zeros((96, 128), F32)
        corners[pl.ds(lo * 8, 24), :] = jnp.zeros((24, 128), F32)
    corners[pl.ds(pl.multiple_of((g + 3) * 8, 8), 8), :] = csend[...]
    for d, there in near:
        @pl.when(there)
        def _(d=d):
            corner_msg(d, g, d).start()


    turned = lax.rem(lane + 1, 128)

    def columns(vs):
        items = [(v, 1) for v in vs]
        while len(items) > 1:
            merged = []
            for n in range(0, len(items) - 1, 2):
                (a, ca), (b, cb) = items[n], items[n + 1]
                merged.append((jnp.where(turned < 2 * ca, a, pltpu.roll(b, 2 * ca, 1)), ca + cb))
            if len(items) % 2:
                merged.append(items[-1])
            items = merged
        return items[0][0]

    even = lax.rem(lane, 2) == 0

    def pack(i, _):
        sides = []
        for r in range(2):
            tiles = [bins_v[pl.ds((2 * i + r) * LVL + m * 8, 8), :] for m in range(NB)]
            sides.append(columns(tiles + [u_v[pl.ds((2 * i + r) * 8, 8), :]]))
        other = pltpu.roll(sides[1], 1, 1)
        send_f[pl.ds(i * 8, 8), :] = jnp.where(even, sides[0], other)
        send_l[pl.ds(i * 8, 8), :] = jnp.where(even, other, sides[0])
        return 0

    lax.fori_loop(0, NL // 2, pack, 0)
    x_copies = [
        pltpu.make_async_remote_copy(src_ref=s, dst_ref=d, send_sem=h_send.at[i], recv_sem=h_recv.at[i], device_id=to, device_id_type=MESH)
        for i, s, d, to in ((3, send_f, halo_r, left), (4, send_l, halo_l, right))
    ]
    for c in x_copies:
        c.start()

    for c in loads[3:]:
        c.wait()

    block = lax.broadcasted_iota(jnp.int32, (64, 64), 0)
    slot = lax.broadcasted_iota(jnp.int32, (64, 64), 1)
    hits = (jnp.broadcast_to(ids_v[...], (64, 64)) == block) & (slot < jnp.broadcast_to(cnt_v[...], (64, 64)))
    marks = jnp.max(jnp.where(hits, 1.0, 0.0), axis=1, keepdims=True)
    col_block = lax.broadcasted_iota(jnp.int32, (16, 128), 1) // 8
    row_block = lax.broadcasted_iota(jnp.int32, (16, 128), 0)
    for bz in range(4):
        wide = jnp.broadcast_to(marks[bz * 16:bz * 16 + 16, :], (16, 128))
        mask_v[pl.ds(bz, 1), :] = jnp.sum(jnp.where(col_block == row_block, wide, 0.0), axis=0, keepdims=True)

    adv[...] = jnp.zeros((NBP * 8, 128), F32)
    coll_v[...] = jnp.zeros((2 * NBP, 3 * NBP), F32)
    pos = lax.broadcasted_iota(jnp.int32, (NB, 3 * NBP), 1)
    row = lax.broadcasted_iota(jnp.int32, (NB, 3 * NBP), 0)
    pick_hi = jnp.where((pos == row) | (pos == row + 2 * NBP), 1.0, 0.0).astype(BF16)
    pick_lo = jnp.where(pos == row + NBP, 1.0, 0.0).astype(BF16)
    for n, ref in enumerate((kern_v, redi_v)):
        hi, lo = split(ref[...])
        coll_v[pl.ds(n * NBP, NB), :] = dot_t(hi, pick_hi) + dot_t(lo, pick_lo)
    for m in range(NB):
        fall_t[pl.ds(m * 8, 8), :] = jnp.broadcast_to(fall_v[:, m:m + 1], (8, 128))

    def level(z, i, r):
        u = u_v[pl.ds(z * 8, 8), :]
        u_pos, u_neg = jnp.maximum(u, 0.0), jnp.minimum(u, 0.0)
        w = w_v[pl.ds(z * 8, 8), :]
        hr = halo_r[pl.ds(i * 8, 8), :]
        pf = prior[pl.ds(i * 8, 8), :]
        base = z * LVL
        for m in range(NB):
            k = 2 * m + r
            kl = (k + 127) % 128
            b = bins_v[pl.ds(base + m * 8, 8), :]
            up = bins_v[pl.ds(base + LVL + m * 8, 8), :]
            nxt = jnp.where(lane == 127, jnp.broadcast_to(hr[:, k:k + 1], (8, 128)), pltpu.roll(b, 127, 1))
            flux = u_pos * b + u_neg * nxt
            prev = jnp.where(lane == 0, jnp.broadcast_to(pf[:, kl:kl + 1], (8, 128)), pltpu.roll(flux, 1, 1))
            c = w - fall_t[pl.ds(m * 8, 8), :]
            top = jnp.maximum(c, 0.0) * b + jnp.minimum(c, 0.0) * up
            s = pl.ds(m * 8, 8)
            adv[s, :] = b - (flux - prev) - (top - fz[s, :])
            fz[s, :] = top
        mark = jnp.broadcast_to(mask_v[pl.ds(z // 8, 1), :], (NBP, 128))
        grow_w = coll_v[pl.ds(0, NBP), :].astype(BF16)
        redi_w = coll_v[pl.ds(NBP, NBP), :].astype(BF16)
        for h in range(4):
            ys = (2 * h, 2 * h + 1)
            v = jnp.concatenate([adv[pl.ds(y, NBP, stride=8), :] for y in ys], axis=1)
            hi, lo = split(v)
            rate = dot(grow_w, jnp.concatenate([hi, hi, lo], axis=0))
            hi, lo = split(v * rate)
            tend = dot(redi_w, jnp.concatenate([hi, hi, lo], axis=0))
            for n, y in enumerate(ys):
                part = slice(128 * n, 128 * n + 128)
                new = v[:, part] + tend[:, part] * mark
                out_v[pl.ds(base + y, NB, stride=8), :] = new[:NB]

    def levels(first, last):
        def step(i, _):
            level(2 * i, i, 0)
            level(2 * i + 1, i, 1)
            return 0
        lax.fori_loop(first, last, step, 0)

    wait_all(0, send1, x1, 9)

    @pl.when(takes_w)
    def _():
        pltpu.make_async_remote_copy(
            src_ref=wtop, dst_ref=wtop, send_sem=w_send, recv_sem=w_recv,
            device_id={"gx": lax.rem(me + 1, NP)}, device_id_type=MESH).wait_recv()

    borders = x1[pl.ds(8, NP, stride=16), :]
    borders = pltpu.roll(borders, 1, 0)
    lane32 = lax.broadcasted_iota(jnp.int32, (32, 128), 1)
    e3 = mats_v[pl.ds(0, 96), :]
    f2 = mats_v[pl.ds(96, 128), :]
    twr = tw_v[:, 0:128]
    twi = tw_v[:, 128:256]
    for h in range(4):
        us = []
        for y in (2 * h, 2 * h + 1):
            xy = x1[pl.ds(y, NP, stride=16), :] - wtop[pl.ds(y, NP, stride=8), :]
            shifted = borders if y == 0 else pltpu.roll(borders, 128 - y, 1)
            xy = xy - jnp.where(lane32 == 0, shifted, 0.0)
            hi, lo = split(xy)
            yy = dot_t(jnp.concatenate([hi, lo, hi], axis=0), e3)
            yr, yi = yy[:, :128], yy[:, 128:]
            us.append(jnp.concatenate([yr * twr - yi * twi, yr * twi + yi * twr], axis=0))
        hi, lo = split(jnp.concatenate(us, axis=1))
        both = dot(f2, hi)
        spec = both[:64] + both[64:] + dot(f2[:64], lo)
        for n, y in enumerate((2 * h, 2 * h + 1)):
            part = slice(128 * n, 128 * n + 128)
            send2[pl.ds(y, NP, stride=16), :] = spec[:32, part]
            send2[pl.ds(8 + y, NP, stride=16), :] = spec[32:, part]
    send_all(1, send2, x2, 16, 16)
    own(send2, x2, 16, 16)

    @pl.when(not_last)
    def _():
        z_up.wait_send()
        w_up.wait_send()
        z_down.wait_recv()

    @pl.when(not_first)
    def _():
        z_up.wait_recv()
        w_up.wait_recv()
        z_down.wait_send()

    for c in x_copies:
        c.wait()

    def prior_step(i, _):
        s = pl.ds(i * 8, 8)
        edge = halo_l[s, :]
        speed = jnp.where(even, jnp.broadcast_to(edge[:, 66:67], (8, 128)), jnp.broadcast_to(edge[:, 65:66], (8, 128)))
        prior[s, :] = jnp.maximum(speed, 0.0) * edge + jnp.minimum(speed, 0.0) * pltpu.roll(send_f[s, :], 127, 1)
        return 0

    lax.fori_loop(0, NL // 2, prior_step, 0)

    w_low = jnp.where(not_first, wlow[...], 0.0)

    def low_face(m, _):
        s = pl.ds(m * 8, 8)
        c = w_low - fall_t[s, :]
        fz[s, :] = jnp.maximum(c, 0.0) * jnp.where(not_first, zlo[s, :], 0.0) + jnp.minimum(c, 0.0) * bins_v[s, :]
        bins_v[pl.ds(NL * LVL + m * 8, 8), :] = jnp.where(not_last, zhi[s, :], 0.0)
        return 0

    lax.fori_loop(0, NB, low_face, 0)


    levels(0, CUT[0])

    wait_all(1, send2, x2, 16)

    def apply_rows(rows):
        accs = [None] * len(rows)
        for j in range(NL):
            s = x2[pl.ds(j * 16, 16), :]
            for n, i in enumerate(rows):
                b = jnp.broadcast_to(binv_v[pl.ds(i * 32 + j, 1), :], (16, 128))
                accs[n] = b * s if accs[n] is None else accs[n] + b * s
        return accs

    low, high = apply_rows((0, 31))
    esend[pl.ds(0, 16), :] = low
    esend[pl.ds(16, 16), :] = high
    edges[pl.ds(pl.multiple_of((g + 3) * 32, 8), 32), :] = esend[...]
    for d, there in near:
        @pl.when(there)
        def _(d=d):
            edge_msg(d, g, d).start()

    def solve_step(t, _):
        rows = [t * 4 + n for n in range(4)]
        for i, acc in zip(rows, apply_rows(rows)):
            send3[pl.ds(i * 16, 16), :] = acc
        return 0

    lax.fori_loop(0, NL // 4, solve_step, 0)
    levels(CUT[0], CUT[1])
    for d, there in near:
        @pl.when(there)
        def _(d=d):
            corner_msg(d, g, d).wait_send()
            corner_msg(d, g + d, -d).wait_recv()
            edge_msg(d, g, d).wait_send()
            edge_msg(d, g + d, -d).wait_recv()

    def e0(d):
        return edges[pl.ds(pl.multiple_of((g + 3 + d) * 32, 8), 16), :]

    def e1(d):
        return edges[pl.ds(pl.multiple_of((g + 3 + d) * 32 + 16, 8), 16), :]

    def corner(d, i):
        return jnp.broadcast_to(corners[pl.ds((g + 3 + d) * 8 + i, 1), :], (16, 128))

    def low_edge(d, over, under):
        return e0(d) + corner(d, 1) * over + corner(d, 0) * under

    def high_edge(d, over, under):
        return e1(d) + corner(d, 3) * over + corner(d, 2) * under

    over = low_edge(1, low_edge(2, e0(3), e1(1)), high_edge(0, e0(1), e1(-1)))
    under = high_edge(-1, low_edge(0, e0(1), e1(-1)), high_edge(-2, e0(-1), e1(-3)))

    def update(t, _):
        for n in range(4):
            i = t * 4 + n
            s = pl.ds(i * 16, 16)
            top = jnp.broadcast_to(binv_v[pl.ds(i * 32 + 31, 1), :], (16, 128))
            bot = jnp.broadcast_to(binv_v[pl.ds(i * 32, 1), :], (16, 128))
            send3[s, :] = send3[s, :] + top * over + bot * under
        return 0

    lax.fori_loop(0, NL // 4, update, 0)
    send_all(2, send3, x3, 16, 16)
    own(send3, x3, 16, 16)

    levels(CUT[1], CUT[2])

    wait_all(2, send3, x3, 16)
    g3 = mats_v[pl.ds(224, 192), :]
    h2 = mats_v[pl.ds(416, 64), :]
    for h in range(4):
        zs = []
        for y in (2 * h, 2 * h + 1):
            s2 = jnp.concatenate([x3[pl.ds(y, NP, stride=16), :], x3[pl.ds(8 + y, NP, stride=16), :]], axis=0)
            hi, lo = split(s2)
            vv = dot_t(jnp.concatenate([hi, lo, hi], axis=0), g3)
            vr, vi = vv[:, :128], vv[:, 128:]
            zs.append(jnp.concatenate([vr * twr + vi * twi, vi * twr - vr * twi], axis=0))
        hi, lo = split(jnp.concatenate(zs, axis=1))
        both = dot(h2, hi)
        pr = both[:32] + both[32:] + dot(h2[:32], lo)
        for n, y in enumerate((2 * h, 2 * h + 1)):
            send4[pl.ds(y, NP, stride=8), :] = pr[:, 128 * n:128 * n + 128]
    send_all(3, send4, pres_v, 8, 8)
    own(send4, pres_v, 8, 8)

    levels(CUT[2], NL // 2)

    @pl.when(not_last)
    def _():
        w_msg(me).wait_send()

    wait_all(3, send4, pres_v, 8)


def write_body(out_v, pres_v, out_h, pres_h, sem):
    copies = [pltpu.make_async_copy(pres_v, pres_h, sem.at[8])]
    for i in range(8):
        s = pl.ds(i * 4 * LVL, 4 * LVL)
        copies.append(pltpu.make_async_copy(out_v.at[s], out_h.at[s], sem.at[i]))
    for c in copies:
        c.start()
    for c in copies:
        c.wait()


CUT = (5, 8, 14)


def body(bins, u, w, fall, kern, redi, ids, counts, binv):
    mats, tw = tables()
    vmem = lambda rows, cols=128, t=F32: pltpu.VMEM((rows, cols), t)
    dma = pltpu.SemaphoreType.DMA
    out, pres = pl.pallas_call(
        kernel_body,
        out_shape=(pltpu.VMEM((NL * LVL, 128), F32), pltpu.VMEM((NL * 8, 128), F32)),
        in_specs=[pl.BlockSpec(memory_space=pltpu.HBM)] * 11,
        out_specs=[pl.BlockSpec(memory_space=pltpu.VMEM)] * 2,
        scratch_shapes=[
            vmem((NL + 1) * LVL), vmem(256), vmem(256), vmem(1024), vmem(480, 256, BF16), vmem(128, 256),
            vmem(NB, NB), vmem(NB, NB), vmem(1, 64, jnp.int32), vmem(1, NB), vmem(1, 1, jnp.int32), vmem(2 * NBP, 3 * NBP), vmem(LVL),
            vmem(512), vmem(512), vmem(512), vmem(512), vmem(512), vmem(512), vmem(256), vmem(256),
            vmem(32), vmem((NG + 6) * 32), vmem(8), vmem((NG + 6) * 8),
            vmem(8), vmem(LVL), vmem(LVL), vmem(128), vmem(128), vmem(128), vmem(128), vmem(128),
            vmem(NBP * 8), vmem(LVL), vmem(8),
            dma((10,)), dma,
            dma((4,)), dma((4,)), dma((7,)), dma((7,)), dma((7,)), dma((7,)), dma((5,)), dma((5,)), dma, dma,
        ],
        compiler_params=pltpu.CompilerParams(collective_id=0, has_side_effects=True, vmem_limit_bytes=62300000),
        name="slab_step",
    )(
        bins.reshape(NL * LVL, 128), u.reshape(256, 128), w.reshape(256, 128), binv.reshape(1024, 128),
        jnp.asarray(mats), jnp.asarray(tw), kern, redi, ids, fall.reshape(1, NB), counts,
    )
    out, pres = pl.pallas_call(
        write_body,
        out_shape=(jax.ShapeDtypeStruct((NL * LVL, 128), F32), jax.ShapeDtypeStruct((NL * 8, 128), F32)),
        in_specs=[pl.BlockSpec(memory_space=pltpu.VMEM)] * 2,
        out_specs=[pl.BlockSpec(memory_space=pl.ANY)] * 2,
        scratch_shapes=[dma((9,))],
        compiler_params=pltpu.CompilerParams(vmem_limit_bytes=1024 * 1024),
        name="write_out",
    )(out, pres)
    return out.reshape(NL, NB, 8, 128), pres.reshape(NL, 8, 128)


def solution(mesh):
    return jax.shard_map(
        body,
        mesh=mesh,
        in_specs=(
            P("gz", None, None, "gx"),
            P("gz", None, "gx"),
            P("gz", None, "gx"),
            P(),
            P(),
            P(),
            P("gz", "gx"),
            P("gz", "gx"),
            P("gz", None, "gx"),
        ),
        out_specs=(P("gz", None, None, "gx"), P("gz", None, "gx")),
        check_vma=False,
    )
```

```python
import functools
import math

import jax
import jax.numpy as jnp
import numpy as np
from jax import lax
from jax.experimental import pallas as pl
from jax.experimental.pallas import tpu as pltpu
from jax.sharding import PartitionSpec as P

F32 = jnp.float32
BF16 = jnp.bfloat16
MESH = pl.DeviceIdType.MESH
NB = 33
NBP = 48
NL = 32
NG = 8
NP = 32
LVL = NB * 8


def halves(x):
    hi = np.asarray(np.asarray(x, np.float32), jnp.bfloat16)
    lo = np.asarray(np.asarray(x - hi.astype(np.float64), np.float32), jnp.bfloat16)
    return hi, lo


def tables():
    p = np.arange(32)
    c = np.arange(128)
    pj = 2.0 * math.pi / 32 * (p[:, None] * c[None, :] % 32)
    cj = 2.0 * math.pi / 4096 * (c[:, None] * c[None, :])
    cos, sin = np.cos(pj), np.sin(pj)
    e_hi, e_lo = halves(np.concatenate([cos, -sin], 1))
    e3 = np.concatenate([e_hi, e_hi, e_lo], 0)
    fwd = np.concatenate([np.concatenate([cos, sin], 1), np.concatenate([-sin, cos], 1)], 0)
    f2 = np.concatenate(halves(fwd), 0)
    g = np.concatenate([np.concatenate([cos, sin], 1), np.concatenate([-sin, cos], 1)], 0)
    g_hi, g_lo = halves(g)
    g3 = np.concatenate([g_hi, g_hi, g_lo], 0)
    h2 = np.concatenate(halves(np.concatenate([cos, -sin], 1) / 4096.0), 0)
    mats = np.concatenate([e3, f2, g3, h2], 0)
    tw = np.concatenate([np.cos(cj), -np.sin(cj)], 1).astype(np.float32)
    return mats, tw


def split(x):
    hi = x.astype(BF16)
    lo = (x - hi.astype(F32)).astype(BF16)
    return hi, lo


def dot(a, b):
    return jnp.dot(a, b, preferred_element_type=F32)


def dot_t(a, b):
    return lax.dot_general(a, b, (((0,), (0,)), ((), ())), preferred_element_type=F32)


def kernel_body(
    bins_h, u_h, w_h, binv_h, mats_h, tw_h, kern_h, redi_h, ids_h, fall_h, cnt_h,
    out_v, pres_v,
    bins_v, u_v, w_v, binv_v, mats_v, tw_v, kern_v, redi_v, ids_v, fall_v, cnt_v, coll_v, fall_t,
    send1, x1, send2, x2, send3, x3, send4, wtop,
    esend, edges, csend, corners,
    wlow, zlo, zhi, send_f, send_l, halo_r, halo_l, prior,
    adv, fz, mask_v,
    in_sem, bin_sem,
    a2a_send, a2a_recv, e_send, e_recv, c_send, c_recv, h_send, h_recv, w_send, w_recv,
):
    me = lax.axis_index("gx")
    g = lax.axis_index("gz")
    right = {"gx": lax.rem(me + 1, NP)}
    left = {"gx": lax.rem(me + NP - 1, NP)}
    above = {"gz": lax.rem(g + 1, NG)}
    below = {"gz": lax.rem(g + NG - 1, NG)}

    lane = lax.broadcasted_iota(jnp.int32, (8, 128), 1)
    sub = lax.broadcasted_iota(jnp.int32, (8, 128), 0)

    barrier = pltpu.get_barrier_semaphore()

    def peer_of(t):
        half = (t + 1) // 2
        odd = lax.rem(t, 2)
        o = 16 + odd * half - (1 - odd) * half
        return lax.rem(me + o, NP)

    def greet(gx, gz):
        pl.semaphore_signal(barrier, inc=1, device_id={"gx": gx, "gz": gz}, device_id_type=MESH)

    def greet_low(o, _):
        greet(o, lax.rem(g + NG - 1, NG))
        return 0

    not_first = g > 0
    not_last = g < NG - 1
    takes_w = (me == 0) & not_first
    near = [(d, (g + d >= 0) & (g + d < NG)) for d in (3, -3, 2, -2, 1, -1)]

    loads = [
        pltpu.make_async_copy(s, d, in_sem.at[i])
        for i, (s, d) in enumerate(
            [(u_h, u_v), (w_h, w_v), (binv_h, binv_v), (mats_h, mats_v), (tw_h, tw_v),
             (kern_h, kern_v), (redi_h, redi_v), (ids_h, ids_v), (fall_h, fall_v), (cnt_h, cnt_v)]
        )
    ]
    loads[0].start()
    loads[1].start()
    for t in range(NP - 1):
        half = (t + 1) // 2
        greet(lax.rem(me + (16 + half if t % 2 else 16 - half), NP), g)
    for d, there in near:
        @pl.when(there)
        def _(d=d):
            greet(me, g + d)

    @pl.when(takes_w)
    def _():
        lax.fori_loop(1, NP, greet_low, 0)

    bin_loads = [
        pltpu.make_async_copy(bins_h.at[pl.ds(i * 4 * LVL, 4 * LVL)], bins_v.at[pl.ds(i * 4 * LVL, 4 * LVL)], bin_sem)
        for i in range(8)
    ]
    for i in range(8):
        bin_loads[i].start()
    for c in loads[2:]:
        c.start()
    loads[0].wait()
    loads[1].wait()

    def tile_div(q, w_under):
        u = u_v[pl.ds(q * 8, 8), :]
        before = jnp.where(lane == 0, 0.0, pltpu.roll(u, 1, 1))
        d = (u - before) + (w_v[pl.ds(q * 8, 8), :] - w_under)
        row = jnp.sum(jnp.where(lane == sub, jnp.broadcast_to(u[:, 127:128], (8, 128)), 0.0), axis=0, keepdims=True)
        send1[pl.ds(q * 16, 8), :] = d
        send1[pl.ds(q * 16 + 8, 8), :] = jnp.broadcast_to(row, (8, 128))

    tile_div(0, jnp.zeros((8, 128), F32))
    for q in range(1, NL):
        tile_div(q, w_v[pl.ds(q * 8 - 8, 8), :])

    @pl.when(jnp.logical_not(takes_w))
    def _():
        wtop[...] = jnp.zeros((256, 128), F32)

    extra = jnp.where(not_last & (me != 0), 1, 0)
    n_near = jnp.minimum(g, 3) + jnp.minimum(NG - 1 - g, 3)
    pl.semaphore_wait(barrier, NP - 1 + n_near + extra)

    def w_msg(p):
        return pltpu.make_async_remote_copy(
            src_ref=w_v.at[pl.ds(248, 8)], dst_ref=wtop.at[pl.ds(pl.multiple_of(p * 8, 8), 8)],
            send_sem=w_send, recv_sem=w_recv, device_id={"gx": me * 0, "gz": lax.rem(g + 1, NG)}, device_id_type=MESH)

    @pl.when(not_last)
    def _():
        w_msg(me).start()

    def msg(stage, src, dst, rows, peer, at):
        s0 = pl.multiple_of(peer * at, 8)
        d0 = pl.multiple_of(me * at, 8)
        return pltpu.make_async_remote_copy(
            src_ref=src.at[pl.ds(s0, rows)], dst_ref=dst.at[pl.ds(d0, rows)],
            send_sem=a2a_send.at[stage], recv_sem=a2a_recv.at[stage],
            device_id={"gx": peer}, device_id_type=MESH)

    def send_all(stage, src, dst, rows, at):
        def step(t, _):
            msg(stage, src, dst, rows, peer_of(t), at).start()
            return 0
        lax.fori_loop(0, NP - 1, step, 0)

    def wait_all(stage, src, dst, rows):
        total = pl.ds(0, (NP - 1) * rows)
        pltpu.make_async_remote_copy(
            src_ref=src.at[total], dst_ref=dst.at[total], send_sem=a2a_send.at[stage], recv_sem=a2a_recv.at[stage],
            device_id={"gx": lax.rem(me + 1, NP)}, device_id_type=MESH).wait()

    def own(src, dst, rows, at):
        m0 = pl.multiple_of(me * at, 8)
        dst[pl.ds(m0, rows), :] = src[pl.ds(m0, rows), :]

    send_all(0, send1, x1, 9, 16)
    own(send1, x1, 16, 16)

    pltpu.make_async_copy(bins_h, bins_v.at[pl.ds(0, NL * LVL)], bin_sem).wait()
    z_up = pltpu.make_async_remote_copy(
        src_ref=bins_v.at[pl.ds(31 * LVL, LVL)], dst_ref=zlo, send_sem=h_send.at[1], recv_sem=h_recv.at[1],
        device_id=above, device_id_type=MESH)
    z_down = pltpu.make_async_remote_copy(
        src_ref=bins_v.at[pl.ds(0, LVL)], dst_ref=zhi, send_sem=h_send.at[2], recv_sem=h_recv.at[2],
        device_id=below, device_id_type=MESH)
    w_up = pltpu.make_async_remote_copy(
        src_ref=w_v.at[pl.ds(248, 8)], dst_ref=wlow, send_sem=h_send.at[0], recv_sem=h_recv.at[0],
        device_id=above, device_id_type=MESH)

    @pl.when(not_last)
    def _():
        w_up.start()
        z_up.start()

    @pl.when(jnp.logical_not(not_first))
    def _():
        wlow[...] = jnp.zeros((8, 128), F32)
        zlo[...] = jnp.zeros((LVL, 128), F32)

    @pl.when(jnp.logical_not(not_last))
    def _():
        zhi[...] = jnp.zeros((LVL, 128), F32)

    loads[2].wait()
    csend[...] = jnp.zeros((8, 128), F32)
    for i, r in enumerate((0, 31, 31 * 32, 31 * 32 + 31)):
        csend[pl.ds(i, 1), :] = binv_v[pl.ds(r, 1), :]

    def corner_msg(d, group, toward):
        return pltpu.make_async_remote_copy(
            src_ref=csend, dst_ref=corners.at[pl.ds(pl.multiple_of((group + 3) * 8, 8), 8)],
            send_sem=c_send.at[d + 3], recv_sem=c_recv.at[toward + 3], device_id={"gz": lax.rem(g + d + NG, NG)}, device_id_type=MESH)

    def edge_msg(d, group, toward):
        first = 16 if abs(d) > 1 and toward > 0 else 0
        rows = 32 if abs(d) == 1 else 16
        return pltpu.make_async_remote_copy(
            src_ref=esend.at[pl.ds(first, rows)], dst_ref=edges.at[pl.ds(pl.multiple_of((group + 3) * 32 + first, 8), rows)],
            send_sem=e_send.at[d + 3], recv_sem=e_recv.at[toward + 3], device_id={"gz": lax.rem(g + d + NG, NG)}, device_id_type=MESH)

    for lo in (0, NG + 3):
        edges[pl.ds(lo * 32, 96), :] = jnp.zeros((96, 128), F32)
        corners[pl.ds(lo * 8, 24), :] = jnp.zeros((24, 128), F32)
    corners[pl.ds(pl.multiple_of((g + 3) * 8, 8), 8), :] = csend[...]
    for d, there in near:
        @pl.when(there)
        def _(d=d):
            corner_msg(d, g, d).start()


    turned = lax.rem(lane + 1, 128)

    def columns(vs):
        items = [(v, 1) for v in vs]
        while len(items) > 1:
            merged = []
            for n in range(0, len(items) - 1, 2):
                (a, ca), (b, cb) = items[n], items[n + 1]
                merged.append((jnp.where(turned < 2 * ca, a, pltpu.roll(b, 2 * ca, 1)), ca + cb))
            if len(items) % 2:
                merged.append(items[-1])
            items = merged
        return items[0][0]

    even = lax.rem(lane, 2) == 0

    def pack(i, _):
        sides = []
        for r in range(2):
            tiles = [bins_v[pl.ds((2 * i + r) * LVL + m * 8, 8), :] for m in range(NB)]
            sides.append(columns(tiles + [u_v[pl.ds((2 * i + r) * 8, 8), :]]))
        other = pltpu.roll(sides[1], 1, 1)
        send_f[pl.ds(i * 8, 8), :] = jnp.where(even, sides[0], other)
        send_l[pl.ds(i * 8, 8), :] = jnp.where(even, other, sides[0])
        return 0

    lax.fori_loop(0, NL // 2, pack, 0)
    x_copies = [
        pltpu.make_async_remote_copy(src_ref=s, dst_ref=d, send_sem=h_send.at[i], recv_sem=h_recv.at[i], device_id=to, device_id_type=MESH)
        for i, s, d, to in ((3, send_f, halo_r, left), (4, send_l, halo_l, right))
    ]
    for c in x_copies:
        c.start()

    for c in loads[3:]:
        c.wait()

    block = lax.broadcasted_iota(jnp.int32, (64, 64), 0)
    slot = lax.broadcasted_iota(jnp.int32, (64, 64), 1)
    hits = (jnp.broadcast_to(ids_v[...], (64, 64)) == block) & (slot < jnp.broadcast_to(cnt_v[...], (64, 64)))
    marks = jnp.max(jnp.where(hits, 1.0, 0.0), axis=1, keepdims=True)
    col_block = lax.broadcasted_iota(jnp.int32, (16, 128), 1) // 8
    row_block = lax.broadcasted_iota(jnp.int32, (16, 128), 0)
    for bz in range(4):
        wide = jnp.broadcast_to(marks[bz * 16:bz * 16 + 16, :], (16, 128))
        mask_v[pl.ds(bz, 1), :] = jnp.sum(jnp.where(col_block == row_block, wide, 0.0), axis=0, keepdims=True)

    adv[...] = jnp.zeros((NBP * 8, 128), F32)
    coll_v[...] = jnp.zeros((2 * NBP, 3 * NBP), F32)
    pos = lax.broadcasted_iota(jnp.int32, (NB, 3 * NBP), 1)
    row = lax.broadcasted_iota(jnp.int32, (NB, 3 * NBP), 0)
    pick_hi = jnp.where((pos == row) | (pos == row + 2 * NBP), 1.0, 0.0).astype(BF16)
    pick_lo = jnp.where(pos == row + NBP, 1.0, 0.0).astype(BF16)
    for n, ref in enumerate((kern_v, redi_v)):
        hi, lo = split(ref[...])
        coll_v[pl.ds(n * NBP, NB), :] = dot_t(hi, pick_hi) + dot_t(lo, pick_lo)
    for m in range(NB):
        fall_t[pl.ds(m * 8, 8), :] = jnp.broadcast_to(fall_v[:, m:m + 1], (8, 128))

    def level(z, i, r):
        u = u_v[pl.ds(z * 8, 8), :]
        u_pos, u_neg = jnp.maximum(u, 0.0), jnp.minimum(u, 0.0)
        w = w_v[pl.ds(z * 8, 8), :]
        hr = halo_r[pl.ds(i * 8, 8), :]
        pf = prior[pl.ds(i * 8, 8), :]
        base = z * LVL
        for m in range(NB):
            k = 2 * m + r
            kl = (k + 127) % 128
            b = bins_v[pl.ds(base + m * 8, 8), :]
            up = bins_v[pl.ds(base + LVL + m * 8, 8), :]
            nxt = jnp.where(lane == 127, jnp.broadcast_to(hr[:, k:k + 1], (8, 128)), pltpu.roll(b, 127, 1))
            flux = u_pos * b + u_neg * nxt
            prev = jnp.where(lane == 0, jnp.broadcast_to(pf[:, kl:kl + 1], (8, 128)), pltpu.roll(flux, 1, 1))
            c = w - fall_t[pl.ds(m * 8, 8), :]
            top = jnp.maximum(c, 0.0) * b + jnp.minimum(c, 0.0) * up
            s = pl.ds(m * 8, 8)
            adv[s, :] = b - (flux - prev) - (top - fz[s, :])
            fz[s, :] = top
        mark = jnp.broadcast_to(mask_v[pl.ds(z // 8, 1), :], (NBP, 128))
        grow_w = coll_v[pl.ds(0, NBP), :].astype(BF16)
        redi_w = coll_v[pl.ds(NBP, NBP), :].astype(BF16)
        for h in range(4):
            ys = (2 * h, 2 * h + 1)
            v = jnp.concatenate([adv[pl.ds(y, NBP, stride=8), :] for y in ys], axis=1)
            hi, lo = split(v)
            rate = dot(grow_w, jnp.concatenate([hi, hi, lo], axis=0))
            hi, lo = split(v * rate)
            tend = dot(redi_w, jnp.concatenate([hi, hi, lo], axis=0))
            for n, y in enumerate(ys):
                part = slice(128 * n, 128 * n + 128)
                new = v[:, part] + tend[:, part] * mark
                out_v[pl.ds(base + y, NB, stride=8), :] = new[:NB]

    def levels(first, last):
        def step(i, _):
            level(2 * i, i, 0)
            level(2 * i + 1, i, 1)
            return 0
        lax.fori_loop(first, last, step, 0)

    wait_all(0, send1, x1, 9)

    @pl.when(takes_w)
    def _():
        pltpu.make_async_remote_copy(
            src_ref=wtop, dst_ref=wtop, send_sem=w_send, recv_sem=w_recv,
            device_id={"gx": lax.rem(me + 1, NP)}, device_id_type=MESH).wait_recv()

    borders = x1[pl.ds(8, NP, stride=16), :]
    borders = pltpu.roll(borders, 1, 0)
    lane32 = lax.broadcasted_iota(jnp.int32, (32, 128), 1)
    e3 = mats_v[pl.ds(0, 96), :]
    f2 = mats_v[pl.ds(96, 128), :]
    twr = tw_v[:, 0:128]
    twi = tw_v[:, 128:256]
    for h in range(4):
        us = []
        for y in (2 * h, 2 * h + 1):
            xy = x1[pl.ds(y, NP, stride=16), :] - wtop[pl.ds(y, NP, stride=8), :]
            shifted = borders if y == 0 else pltpu.roll(borders, 128 - y, 1)
            xy = xy - jnp.where(lane32 == 0, shifted, 0.0)
            hi, lo = split(xy)
            yy = dot_t(jnp.concatenate([hi, lo, hi], axis=0), e3)
            yr, yi = yy[:, :128], yy[:, 128:]
            us.append(jnp.concatenate([yr * twr - yi * twi, yr * twi + yi * twr], axis=0))
        hi, lo = split(jnp.concatenate(us, axis=1))
        both = dot(f2, hi)
        spec = both[:64] + both[64:] + dot(f2[:64], lo)
        for n, y in enumerate((2 * h, 2 * h + 1)):
            part = slice(128 * n, 128 * n + 128)
            send2[pl.ds(y, NP, stride=16), :] = spec[:32, part]
            send2[pl.ds(8 + y, NP, stride=16), :] = spec[32:, part]
    send_all(1, send2, x2, 16, 16)
    own(send2, x2, 16, 16)

    @pl.when(not_last)
    def _():
        z_up.wait_send()
        w_up.wait_send()

    @pl.when(not_first)
    def _():
        z_up.wait_recv()
        w_up.wait_recv()

    for c in x_copies:
        c.wait()

    def prior_step(i, _):
        s = pl.ds(i * 8, 8)
        edge = halo_l[s, :]
        speed = jnp.where(even, jnp.broadcast_to(edge[:, 66:67], (8, 128)), jnp.broadcast_to(edge[:, 65:66], (8, 128)))
        prior[s, :] = jnp.maximum(speed, 0.0) * edge + jnp.minimum(speed, 0.0) * pltpu.roll(send_f[s, :], 127, 1)
        return 0

    lax.fori_loop(0, NL // 2, prior_step, 0)

    w_low = jnp.where(not_first, wlow[...], 0.0)

    def low_face(m, _):
        s = pl.ds(m * 8, 8)
        c = w_low - fall_t[s, :]
        fz[s, :] = jnp.maximum(c, 0.0) * jnp.where(not_first, zlo[s, :], 0.0) + jnp.minimum(c, 0.0) * bins_v[s, :]
        return 0

    lax.fori_loop(0, NB, low_face, 0)


    levels(0, CUT[0])

    wait_all(1, send2, x2, 16)

    def apply_rows(rows):
        accs = [None] * len(rows)
        for j in range(NL):
            s = x2[pl.ds(j * 16, 16), :]
            for n, i in enumerate(rows):
                b = jnp.broadcast_to(binv_v[pl.ds(i * 32 + j, 1), :], (16, 128))
                accs[n] = b * s if accs[n] is None else accs[n] + b * s
        return accs

    low, high = apply_rows((0, 31))
    esend[pl.ds(0, 16), :] = low
    esend[pl.ds(16, 16), :] = high
    edges[pl.ds(pl.multiple_of((g + 3) * 32, 8), 32), :] = esend[...]
    for d, there in near:
        @pl.when(there)
        def _(d=d):
            edge_msg(d, g, d).start()

    def solve_step(t, _):
        rows = [t * 4 + n for n in range(4)]
        for i, acc in zip(rows, apply_rows(rows)):
            send3[pl.ds(i * 16, 16), :] = acc
        return 0

    lax.fori_loop(0, NL // 4, solve_step, 0)
    @pl.when(not_first)
    def _():
        z_down.start()

    levels(CUT[0], CUT[1])
    for d, there in near:
        @pl.when(there)
        def _(d=d):
            corner_msg(d, g, d).wait_send()
            corner_msg(d, g + d, -d).wait_recv()
            edge_msg(d, g, d).wait_send()
            edge_msg(d, g + d, -d).wait_recv()

    def e0(d):
        return edges[pl.ds(pl.multiple_of((g + 3 + d) * 32, 8), 16), :]

    def e1(d):
        return edges[pl.ds(pl.multiple_of((g + 3 + d) * 32 + 16, 8), 16), :]

    def corner(d, i):
        return jnp.broadcast_to(corners[pl.ds((g + 3 + d) * 8 + i, 1), :], (16, 128))

    def low_edge(d, over, under):
        return e0(d) + corner(d, 1) * over + corner(d, 0) * under

    def high_edge(d, over, under):
        return e1(d) + corner(d, 3) * over + corner(d, 2) * under

    over = low_edge(1, low_edge(2, e0(3), e1(1)), high_edge(0, e0(1), e1(-1)))
    under = high_edge(-1, low_edge(0, e0(1), e1(-1)), high_edge(-2, e0(-1), e1(-3)))

    def update(t, _):
        for n in range(4):
            i = t * 4 + n
            s = pl.ds(i * 16, 16)
            top = jnp.broadcast_to(binv_v[pl.ds(i * 32 + 31, 1), :], (16, 128))
            bot = jnp.broadcast_to(binv_v[pl.ds(i * 32, 1), :], (16, 128))
            send3[s, :] = send3[s, :] + top * over + bot * under
        return 0

    lax.fori_loop(0, NL // 4, update, 0)
    send_all(2, send3, x3, 16, 16)
    own(send3, x3, 16, 16)

    levels(CUT[1], CUT[2])

    wait_all(2, send3, x3, 16)
    g3 = mats_v[pl.ds(224, 192), :]
    h2 = mats_v[pl.ds(416, 64), :]
    for h in range(4):
        zs = []
        for y in (2 * h, 2 * h + 1):
            s2 = jnp.concatenate([x3[pl.ds(y, NP, stride=16), :], x3[pl.ds(8 + y, NP, stride=16), :]], axis=0)
            hi, lo = split(s2)
            vv = dot_t(jnp.concatenate([hi, lo, hi], axis=0), g3)
            vr, vi = vv[:, :128], vv[:, 128:]
            zs.append(jnp.concatenate([vr * twr + vi * twi, vi * twr - vr * twi], axis=0))
        hi, lo = split(jnp.concatenate(zs, axis=1))
        both = dot(h2, hi)
        pr = both[:32] + both[32:] + dot(h2[:32], lo)
        for n, y in enumerate((2 * h, 2 * h + 1)):
            send4[pl.ds(y, NP, stride=8), :] = pr[:, 128 * n:128 * n + 128]
    send_all(3, send4, pres_v, 8, 8)
    own(send4, pres_v, 8, 8)

    @pl.when(not_last)
    def _():
        z_down.wait_recv()

    @pl.when(not_first)
    def _():
        z_down.wait_send()

    def top_level(m, _):
        s = pl.ds(m * 8, 8)
        bins_v[pl.ds(NL * LVL + m * 8, 8), :] = jnp.where(not_last, zhi[s, :], 0.0)
        return 0

    lax.fori_loop(0, NB, top_level, 0)
    levels(CUT[2], NL // 2)

    @pl.when(not_last)
    def _():
        w_msg(me).wait_send()

    wait_all(3, send4, pres_v, 8)


def write_body(out_v, pres_v, out_h, pres_h, sem):
    copies = [pltpu.make_async_copy(pres_v, pres_h, sem.at[8])]
    for i in range(8):
        s = pl.ds(i * 4 * LVL, 4 * LVL)
        copies.append(pltpu.make_async_copy(out_v.at[s], out_h.at[s], sem.at[i]))
    for c in copies:
        c.start()
    for c in copies:
        c.wait()


CUT = (5, 8, 14)


def body(bins, u, w, fall, kern, redi, ids, counts, binv):
    mats, tw = tables()
    vmem = lambda rows, cols=128, t=F32: pltpu.VMEM((rows, cols), t)
    dma = pltpu.SemaphoreType.DMA
    out, pres = pl.pallas_call(
        kernel_body,
        out_shape=(pltpu.VMEM((NL * LVL, 128), F32), pltpu.VMEM((NL * 8, 128), F32)),
        in_specs=[pl.BlockSpec(memory_space=pltpu.HBM)] * 11,
        out_specs=[pl.BlockSpec(memory_space=pltpu.VMEM)] * 2,
        scratch_shapes=[
            vmem((NL + 1) * LVL), vmem(256), vmem(256), vmem(1024), vmem(480, 256, BF16), vmem(128, 256),
            vmem(NB, NB), vmem(NB, NB), vmem(1, 64, jnp.int32), vmem(1, NB), vmem(1, 1, jnp.int32), vmem(2 * NBP, 3 * NBP), vmem(LVL),
            vmem(512), vmem(512), vmem(512), vmem(512), vmem(512), vmem(512), vmem(256), vmem(256),
            vmem(32), vmem((NG + 6) * 32), vmem(8), vmem((NG + 6) * 8),
            vmem(8), vmem(LVL), vmem(LVL), vmem(128), vmem(128), vmem(128), vmem(128), vmem(128),
            vmem(NBP * 8), vmem(LVL), vmem(8),
            dma((10,)), dma,
            dma((4,)), dma((4,)), dma((7,)), dma((7,)), dma((7,)), dma((7,)), dma((5,)), dma((5,)), dma, dma,
        ],
        compiler_params=pltpu.CompilerParams(collective_id=0, has_side_effects=True, vmem_limit_bytes=62300000),
        name="slab_step",
    )(
        bins.reshape(NL * LVL, 128), u.reshape(256, 128), w.reshape(256, 128), binv.reshape(1024, 128),
        jnp.asarray(mats), jnp.asarray(tw), kern, redi, ids, fall.reshape(1, NB), counts,
    )
    out, pres = pl.pallas_call(
        write_body,
        out_shape=(jax.ShapeDtypeStruct((NL * LVL, 128), F32), jax.ShapeDtypeStruct((NL * 8, 128), F32)),
        in_specs=[pl.BlockSpec(memory_space=pltpu.VMEM)] * 2,
        out_specs=[pl.BlockSpec(memory_space=pl.ANY)] * 2,
        scratch_shapes=[dma((9,))],
        compiler_params=pltpu.CompilerParams(vmem_limit_bytes=1024 * 1024),
        name="write_out",
    )(out, pres)
    return out.reshape(NL, NB, 8, 128), pres.reshape(NL, 8, 128)


def solution(mesh):
    return jax.shard_map(
        body,
        mesh=mesh,
        in_specs=(
            P("gz", None, None, "gx"),
            P("gz", None, "gx"),
            P("gz", None, "gx"),
            P(),
            P(),
            P(),
            P("gz", "gx"),
            P("gz", "gx"),
            P("gz", None, "gx"),
        ),
        out_specs=(P("gz", None, None, "gx"), P("gz", None, "gx")),
        check_vma=False,
    )
```
